32 devices in a mesh: sec: 4 (over y, x), dom: 8 (over z, core).
Axes of the slice: x: 2, y: 2, z: 4, core: 2. Of those that a mesh axis runs over, the one named last changes fastest.
Arguments:
- disp_coarse: float32 [4096], P('dom'), may hold values from -6 to 6
- support_ids: int32 [4, 8, 4], P('sec', 'dom'), may hold values from 0 to 7, all different within a row
- rbf_weights: bfloat16 [4, 8, 4, 512, 64], P('sec', 'dom'), may hold values from -0.125 to 0.125
- flow: float32 [4, 4, 512, 256], P('sec', None, 'dom'), may hold values from -6 to 6
- pivots: int32 [4096], replicated, may hold values from 0 to 4095, each once
- lower_inverse: float32 [4096, 4096], P('dom'), as said below
- upper_inverse: float32 [4096, 4096], P('dom'), as said below
Outputs:
- new_flow: float32 [4, 4, 512, 256], P('sec', None, 'dom')
- new_disp: float32 [4096], P('dom')
The draws below stay inside these ranges and needn't reach their ends.
Inputs may be any that keep to these rules, and one draw needn't show every extreme that they name: `support_ids`: each row names 4 different structure blocks; every block is named by some row. `pivots`: each index once. `lower_inverse`: unit lower triangular. `upper_inverse`: upper triangular with a positive diagonal.
All inputs are finite; a program needn't handle non-finite values.
Results may differ from the reference program's by a relative error of at most 0.00035.
Values may be sent and summed in bfloat16 or wider, within the bound.
No kernel may reach another device: no remote copies, remote signals or barrier semaphores. Data moves between devices by JAX's collectives and lax.ppermute only.
A program may use at most 64 MiB of HBM per device.

```python
import math
import jax
import jax.numpy as jnp
from jax import lax

FRONT = 4096
K = 4
ITERS = 4
CZ = 64
CY = 256
SDOF = 512
ZALL = 512
N_SEC = 4
N_DOM = 8


def draw_lower_inverse(key, part):
    rows = lax.broadcasted_iota(jnp.int32, (FRONT, FRONT), 0)
    cols = lax.broadcasted_iota(jnp.int32, (FRONT, FRONT), 1)
    noise = 1.5 * jnp.clip(jax.random.normal(key, (FRONT, FRONT), jnp.float32), -4.0, 4.0)
    scaled = noise / math.sqrt(FRONT)
    return jnp.where(cols < rows, scaled, jnp.where(cols == rows, 1.0, 0.0)).astype(jnp.float32)


def draw_upper_inverse(key, part):
    diag_key, noise_key = jax.random.split(key)
    rows = lax.broadcasted_iota(jnp.int32, (FRONT, FRONT), 0)
    cols = lax.broadcasted_iota(jnp.int32, (FRONT, FRONT), 1)
    diagonal = jnp.exp(jax.random.uniform(diag_key, (FRONT,), jnp.float32, math.log(0.5), math.log(2.0)))
    noise = 1.5 * jnp.clip(jax.random.normal(noise_key, (FRONT, FRONT), jnp.float32), -4.0, 4.0)
    scaled = noise / math.sqrt(FRONT)
    return jnp.where(cols > rows, scaled, jnp.where(cols == rows, diagonal[:, None], 0.0)).astype(jnp.float32)


def steps_of(rng, dims, shards, smallest, top_value):
    gain, own = 1.0, jax.random.fold_in(rng, 6)
    for axis_at, blocks in shards:
        steps = jnp.exp(jax.random.uniform(jax.random.fold_in(own, axis_at), (blocks,), jnp.float32, smallest / len(shards), top_value / len(shards)))
        gain = gain * jnp.repeat(steps, dims[axis_at] // blocks).reshape([-1 if axis == axis_at else 1 for axis in range(len(dims))])
    return gain


def picks_of(key, rows, amount, top, lift):
    sequence = jax.random.permutation(jax.random.fold_in(key, 1), amount)
    favour = sequence
    for power in range(3):
        favour = favour * favour // amount
    favour = favour * lift // amount
    lots = jax.random.randint(jax.random.fold_in(key, 2), (rows, amount), 0, 4096) + favour
    sure = jax.random.permutation(jax.random.fold_in(key, 3), rows)[jnp.arange(amount) % rows]
    lots = jnp.where(jnp.arange(rows)[:, None] == sure[None, :], 1 << 14, lots)
    score = lots * amount + jnp.arange(amount)
    return lax.top_k(score.astype(jnp.int32), top)[1].astype(jnp.int32)


def centred(rng, dims, deviation, limit, pieces=(), held_as=jnp.bfloat16):
    result = jax.random.normal(rng, dims, jnp.float32) * deviation
    if len(pieces) > 0:
        result = steps_of(rng, dims, pieces, -0.22, 0.18) * result
    return jnp.clip(result, min=-limit, max=limit).astype(held_as)


def setup_inputs(seed: int = 0) -> dict:
    seeds = jax.random.split(jax.random.key(seed), 8)
    return {
        "disp_coarse": centred(seeds[0], (FRONT,), 1.0, 6.0, ((0, 8),), jnp.float32),
        "support_ids": picks_of(seeds[1], N_SEC * N_DOM, N_DOM, K, 8192).reshape((N_SEC, N_DOM, K)),
        "rbf_weights": centred(seeds[2], (N_SEC, N_DOM, K, SDOF, CZ), (K * SDOF) ** -0.5, 0.125, ((0, 4), (1, 8))),
        "flow": centred(seeds[3], (N_SEC, 4, ZALL, CY), 1.0, 6.0, ((0, 4), (2, 8)), jnp.float32),
        "pivots": jax.random.permutation(seeds[4], FRONT).astype(jnp.int32),
        "lower_inverse": draw_lower_inverse(jax.random.fold_in(seeds[7], 71), 0),
        "upper_inverse": draw_upper_inverse(jax.random.fold_in(seeds[7], 71), 0),
    }


COURANT = 0.4
MACH = 0.5
DISSIPATION = 0.03125
FACE_AREA = 0.125


def stencil(padded):
    z_extent = padded.shape[1]
    y_extent = padded.shape[2]
    y_padded = jnp.pad(padded, ((0, 0), (0, 0), (2, 2)))

    def zshift(offset):
        return y_padded[:, 2 + offset:z_extent - 2 + offset, 2:y_extent + 2]

    def yshift(offset):
        return y_padded[:, 2:z_extent - 2, 2 + offset:y_extent + 2 + offset]

    centre = zshift(0)
    z_slope = 0.5 * (zshift(1) - zshift(-1))
    y_slope = 0.5 * (yshift(1) - yshift(-1))
    z_fourth = zshift(2) - 4.0 * zshift(1) + 6.0 * centre - 4.0 * zshift(-1) + zshift(-2)
    y_fourth = yshift(2) - 4.0 * yshift(1) + 6.0 * centre - 4.0 * yshift(-1) + yshift(-2)
    damping = DISSIPATION * (z_fourth + y_fourth)
    density = centre[0] - COURANT * (MACH * z_slope[0] + z_slope[2] + y_slope[3]) - damping[0]
    pressure = centre[1] - COURANT * (MACH * z_slope[1] + z_slope[2] + y_slope[3]) - damping[1]
    along = centre[2] - COURANT * (MACH * z_slope[2] + z_slope[1]) - damping[2]
    normal = centre[3] - COURANT * (MACH * z_slope[3] + y_slope[1]) - damping[3]
    return jnp.stack([density, pressure, along, normal])


def reference(disp_coarse, support_ids, rbf_weights, flow, pivots, lower_inverse, upper_inverse):
    coarse_table = disp_coarse.astype(jnp.bfloat16).reshape(N_DOM, SDOF)

    def one_section(packed):
        flow_sec, ids_sec, weights_sec = packed
        picked = coarse_table[ids_sec.astype(jnp.int32)]
        wall_motion = jnp.einsum('dkj,dkjz->dz', picked.astype(jnp.float32), weights_sec.astype(jnp.float32)).reshape(ZALL)
        fields = flow_sec.at[3, :, 0].set(wall_motion)
        for sweep_index in range(ITERS):
            padded = jnp.concatenate([fields[:, -2:], fields, fields[:, :2]], axis=1)
            fields = stencil(padded)
        push = (FACE_AREA * fields[1, :, 0]).astype(jnp.bfloat16).reshape(N_DOM, CZ)
        terms = jnp.einsum('dkjz,dz->dkj', weights_sec.astype(jnp.float32), push.astype(jnp.float32))
        onehot = (ids_sec[:, :, None] == jnp.arange(N_DOM, dtype=jnp.int32)[None, None, :]).astype(jnp.float32)
        dense = jnp.einsum('dkb,dkj->bj', onehot, terms, precision=lax.Precision.HIGHEST)
        return fields, dense

    new_flow, denses = lax.map(one_section, (flow, support_ids, rbf_weights))
    forces = jnp.sum(denses, axis=0).reshape(FRONT)
    permuted = jnp.take(forces, pivots, axis=0)
    lower_part = jnp.dot(lower_inverse, permuted, precision=lax.Precision.HIGHEST)
    solved = jnp.dot(upper_inverse, lower_part, precision=lax.Precision.HIGHEST)
    new_disp = 0.5 * disp_coarse + 0.5 * solved
    return new_flow, new_disp
```

```python
import functools

import jax
import jax.numpy as jnp
from jax import lax
from jax.experimental import pallas as pl
from jax.experimental.pallas import tpu as pltpu
from jax.sharding import PartitionSpec as P

ITERS = 4
REACH = 2


COURANT = 0.4
MACH = 0.5
DISSIPATION = 0.03125
FACE_AREA = 0.125

LANES = 128
SUB = 8


def padded_2(cells, sides, width):
    for axis, dim in sides:
        count = lax.axis_size(axis)
        head = lax.slice_in_dim(cells, 0, width, axis=dim)
        tail = lax.slice_in_dim(cells, cells.shape[dim] - width, cells.shape[dim], axis=dim)
        cells = jnp.concatenate(
            [
                lax.ppermute(tail, axis, [(i, (i + 1) % count) for i in range(count)]),
                cells,
                lax.ppermute(head, axis, [((i + 1) % count, i) for i in range(count)]),
            ],
            axis=dim,
        )
    return cells


def stencil(padded):
    z_extent = padded.shape[1]
    y_extent = padded.shape[2]
    y_padded = jnp.pad(padded, ((0, 0), (0, 0), (2, 2)))

    def zshift(offset):
        return y_padded[:, 2 + offset : z_extent - 2 + offset, 2 : y_extent + 2]

    def yshift(offset):
        return y_padded[:, 2 : z_extent - 2, 2 + offset : y_extent + 2 + offset]

    centre = zshift(0)
    z_slope = 0.5 * (zshift(1) - zshift(-1))
    y_slope = 0.5 * (yshift(1) - yshift(-1))
    z_fourth = zshift(2) - 4.0 * zshift(1) + 6.0 * centre - 4.0 * zshift(-1) + zshift(-2)
    y_fourth = yshift(2) - 4.0 * yshift(1) + 6.0 * centre - 4.0 * yshift(-1) + yshift(-2)
    damping = DISSIPATION * (z_fourth + y_fourth)
    density = centre[0] - COURANT * (MACH * z_slope[0] + z_slope[2] + y_slope[3]) - damping[0]
    pressure = centre[1] - COURANT * (MACH * z_slope[1] + z_slope[2] + y_slope[3]) - damping[1]
    along = centre[2] - COURANT * (MACH * z_slope[2] + z_slope[1]) - damping[2]
    normal = centre[3] - COURANT * (MACH * z_slope[3] + y_slope[1]) - damping[3]
    return jnp.stack([density, pressure, along, normal])


def with_rims(fields):
    return padded_2(fields, (("dom", 1),), 2)


def shards(disp_coarse, support_ids, rbf_weights, flow, pivots, lower_inverse, upper_inverse):
    block_size = disp_coarse.shape[0]
    domains = lax.axis_size("dom")
    coarse_table = lax.all_gather(
        disp_coarse.astype(jnp.bfloat16), "dom", axis=0, tiled=True
    ).reshape(domains, block_size)
    support = support_ids[0, 0]
    weights = rbf_weights[0, 0]
    matches = support[:, None] == lax.broadcasted_iota(jnp.int32, (support.shape[0], domains), 1)
    choose = matches.astype(jnp.bfloat16)
    picked = jnp.dot(choose, coarse_table, preferred_element_type=jnp.float32).astype(jnp.bfloat16)
    wall_motion = jnp.einsum("kj,kjz->z", picked, weights, preferred_element_type=jnp.float32)
    fields = flow[0].at[3, :, 0].set(wall_motion)
    for sweep_index in range(ITERS):
        fields = stencil(with_rims(fields))
    push = (FACE_AREA * fields[1, :, 0]).astype(jnp.bfloat16)
    terms = jnp.einsum("kjz,z->kj", weights, push, preferred_element_type=jnp.float32)
    dense = jnp.einsum(
        "kb,kj->bj", matches.astype(jnp.float32), terms, precision=lax.Precision.HIGHEST
    )
    owned = lax.psum_scatter(dense, "dom", scatter_dimension=0, tiled=True)
    owned = lax.psum(owned, "sec")
    forces = lax.all_gather(owned, "dom", axis=0, tiled=True).reshape(-1)
    permuted = jnp.take(forces, pivots, axis=0)
    lower_part = jnp.dot(lower_inverse, permuted, precision=lax.Precision.HIGHEST)
    middle = lax.all_gather(lower_part, "dom", axis=0, tiled=True)
    solved = jnp.dot(upper_inverse, middle, precision=lax.Precision.HIGHEST)
    new_disp = 0.5 * disp_coarse + 0.5 * solved
    return (fields[None], new_disp)


def lane_index(shape):
    return lax.broadcasted_iota(jnp.int32, shape, 1)


def sweep(load, lanes, comps):
    shape = load(0, 0).shape
    lane = lane_index(shape)
    width = shape[1]

    def down(f, n):
        return jnp.where(lane >= n, pltpu.roll(f, n, 1), 0.0)

    def up(f, n):
        return jnp.where(lane < width - n, pltpu.roll(f, width - n, 1), 0.0)

    centre = [load(c, 0) for c in range(4)]
    need_y = set(comps) | ({3} if 0 in comps or 1 in comps else set()) | ({1} if 3 in comps else set())
    y_plus = {c: up(centre[c], 1) for c in need_y}
    y_minus = {c: down(centre[c], 1) for c in need_y}
    z_plus = [load(c, 1) for c in range(4)]
    z_minus = [load(c, -1) for c in range(4)]

    def z_slope(c):
        return 0.5 * (z_plus[c] - z_minus[c])

    def y_slope(c):
        return 0.5 * (y_plus[c] - y_minus[c])

    def damping(c):
        near = z_plus[c] + z_minus[c] + y_plus[c] + y_minus[c]
        far = load(c, 2) + load(c, -2) + up(centre[c], 2) + down(centre[c], 2)
        return DISSIPATION * (far - 4.0 * near + 12.0 * centre[c])

    out = {}
    if 0 in comps or 1 in comps:
        spread = z_slope(2) + y_slope(3)
    if 0 in comps:
        out[0] = centre[0] - COURANT * (MACH * z_slope(0) + spread) - damping(0)
    if 1 in comps:
        out[1] = centre[1] - COURANT * (MACH * z_slope(1) + spread) - damping(1)
    if 2 in comps:
        out[2] = centre[2] - COURANT * (MACH * z_slope(2) + z_slope(1)) - damping(2)
    if 3 in comps:
        out[3] = centre[3] - COURANT * (MACH * z_slope(3) + y_slope(1)) - damping(3)
    return out


def pack_body(halo, me_ref, ids_ref, flow_ref, wt_ref, near_ref, far_ref, own_ref):
    odd = me_ref[0] % 2 == 1
    comps, cells, width = flow_ref.shape
    count = wt_ref.shape[0]
    halves = wt_ref.shape[2] // width
    at = 0
    for c in range(comps):
        head = flow_ref[c, 0:halo, :]
        tail = flow_ref[c, cells - halo : cells, :]
        near_ref[at : at + halo, :] = jnp.where(odd, head, tail)
        far_ref[at : at + halo, :] = jnp.where(odd, tail, head)
        at += halo
    for k in range(count):
        both = wt_ref[k].astype(jnp.float32)
        head, tail = both[0:halo], both[cells - halo : cells]
        near = jnp.where(odd, head, tail)
        far = jnp.where(odd, tail, head)
        for h in range(halves):
            near_ref[at : at + halo, :] = near[:, h * width : (h + 1) * width]
            far_ref[at : at + halo, :] = far[:, h * width : (h + 1) * width]
            at += halo
    row = lax.broadcasted_iota(jnp.int32, (SUB, width), 0)
    ids = jnp.full((SUB, width), -1, jnp.int32)
    for k in range(count):
        ids = jnp.where(row == k, ids_ref[k], ids)
    ids = ids.astype(jnp.float32)
    near_ref[at : at + SUB, :] = ids
    far_ref[at : at + SUB, :] = ids
    own_ref[...] = ids[:, 0:LANES]


def wall_body(
    halo, me_ref, ids_ref, mine_ref, theirs_ref, own_ref, near_ref, far_ref, flow_ref, wt_ref,
    wall_ref, dense_ref, ping, pong,
):
    me = me_ref[0]
    odd = me % 2
    chips = mine_ref.shape[0]
    comps, cells, width = flow_ref.shape
    count, _, block = wt_ref.shape
    halves = block // width
    ids_at = halo * (comps + count * halves)

    slot = lax.broadcasted_iota(jnp.int32, (SUB * 3, 2 * chips), 1)
    chip = (me // 2) ^ (slot % chips)
    core = odd ^ (slot // chips)
    block_of = (2 * chip + core).astype(jnp.float32)
    ids = jnp.concatenate(
        [own_ref[:, 0:1], near_ref[ids_at : ids_at + SUB, 0:1], far_ref[ids_at : ids_at + SUB, 0:1]],
        axis=0,
    )
    choose = (ids == block_of).astype(jnp.bfloat16)
    table = jnp.concatenate([mine_ref[...], theirs_ref[...]], axis=0).astype(jnp.bfloat16)
    picked = jnp.dot(choose, table, preferred_element_type=jnp.float32)

    own = jnp.zeros((cells, LANES), jnp.float32)
    edge = [jnp.zeros((halo, LANES), jnp.float32) for _ in range(2)]
    for k in range(count):
        weights = wt_ref[k].astype(jnp.float32)
        for q in range(0, block, LANES):
            own += weights[:, q : q + LANES] * picked[k : k + 1, q : q + LANES]
            rows = halo * (comps + k * halves + q // width)
            for e, ref in enumerate((near_ref, far_ref)):
                edge[e] += (
                    ref[rows : rows + halo, q % width : q % width + LANES]
                    * picked[SUB * (e + 1) + k : SUB * (e + 1) + k + 1, q : q + LANES]
                )
    own = jnp.sum(own, axis=1, keepdims=True)
    near, far = [jnp.sum(e, axis=1, keepdims=True) for e in edge]
    is_odd = odd == 1
    walls = [
        (SUB, jnp.where(is_odd, near, far)),
        (SUB + halo, own),
        (SUB + halo + cells, jnp.where(is_odd, far, near)),
    ]
    lane = lane_index((1, LANES))
    for at, column in walls:
        rows = column.shape[0]
        column = jnp.broadcast_to(column, (rows, LANES))
        wall_ref[at - SUB : at - SUB + rows, :] = column
        for c in range(comps):
            if rows == cells:
                part = flow_ref[c, :, 0:LANES]
            else:
                a = near_ref[c * halo : (c + 1) * halo, 0:LANES]
                b = far_ref[c * halo : (c + 1) * halo, 0:LANES]
                part = jnp.where(is_odd, a, b) if at == SUB else jnp.where(is_odd, b, a)
            if c == comps - 1:
                part = jnp.where(lane == 0, column, part)
            ping[c, at : at + rows, :] = part

    extent = cells + 2 * halo
    src, dst = ping, pong
    for index in range(ITERS - 1):
        out = sweep(lambda c, o: src[c, SUB + o : SUB + o + extent, :], LANES, (1, 2, 3))
        for c, value in out.items():
            dst[c, SUB : SUB + extent, :] = value
        src, dst = dst, src
    at = SUB + halo
    pressure = sweep(lambda c, o: src[c, at + o : at + o + cells, :], LANES, (1,))[1]
    push = (FACE_AREA * pressure[:, 0:1]).astype(jnp.bfloat16).astype(jnp.float32)
    push = jnp.broadcast_to(push, (cells, LANES))
    dense_ref[...] = jnp.zeros_like(dense_ref)
    for k in range(count):
        weights = wt_ref[k].astype(jnp.float32)
        terms = [
            jnp.sum(weights[:, q : q + LANES] * push, axis=0, keepdims=True)
            for q in range(0, block, LANES)
        ]
        dense_ref[pl.ds(ids_ref[k], 1), :] = jnp.concatenate(terms, axis=1)


def flow_body(halo, me_ref, near_ref, far_ref, flow_ref, wall_ref, out_ref, ping, pong):
    is_odd = me_ref[0] % 2 == 1
    comps, cells, width = flow_ref.shape
    lane = lane_index((1, width))
    for c in range(comps):
        near = near_ref[c * halo : (c + 1) * halo, :]
        far = far_ref[c * halo : (c + 1) * halo, :]
        parts = [
            (0, jnp.where(is_odd, near, far)),
            (halo, flow_ref[c]),
            (halo + cells, jnp.where(is_odd, far, near)),
        ]
        for at, part in parts:
            rows = part.shape[0]
            if c == comps - 1:
                part = jnp.where(lane == 0, wall_ref[at : at + rows, 0:1], part)
            ping[c, SUB + at : SUB + at + rows, :] = part
    src, dst = ping, pong
    extent = cells + 2 * halo
    for index in range(ITERS):
        last = index == ITERS - 1
        first = halo if last else 0
        total = cells if last else extent
        step = 16
        for at in range(first, first + total, step):
            base = SUB + at
            out = sweep(lambda c, o: src[c, base + o : base + o + step, :], width, (0, 1, 2, 3))
            for c, value in out.items():
                if last:
                    out_ref[c, at - halo : at - halo + step, :] = value
                else:
                    dst[c, base : base + step, :] = value
        src, dst = dst, src


def front_product(front_ref, row_of):
    rows, columns = front_ref.shape
    spread = [jnp.broadcast_to(row_of(c), (SUB, LANES)) for c in range(columns // LANES)]
    out = []
    for top in range(0, rows, LANES):
        parts = []
        for at in range(top, top + LANES, SUB):
            total = None
            for c in range(columns // LANES):
                term = front_ref[at : at + SUB, c * LANES : (c + 1) * LANES] * spread[c]
                total = term if total is None else total + term
            parts.append(total)
        out.append(jnp.sum(jnp.concatenate(parts, axis=0).T, axis=0, keepdims=True))
    return jnp.concatenate(out, axis=1)


def lower_body(parts, *refs):
    pieces = refs[:parts]
    pivots_ref, front_ref, out_ref, table, permuted = refs[parts:]
    total = pieces[0][...]
    for ref in pieces[1:]:
        total = total + ref[...]
    table[...] = total
    block = table.shape[1]
    per_block = block // LANES
    pivot = pivots_ref[...]
    shift = LANES.bit_length() - 1
    row = jnp.right_shift(pivot, shift)
    lane = jnp.bitwise_and(pivot, LANES - 1)
    got = jnp.zeros(pivot.shape, jnp.float32)
    for r in range(pivot.shape[0]):
        q = (r % per_block) * LANES
        source = jnp.broadcast_to(
            table[r // per_block : r // per_block + 1, q : q + LANES], pivot.shape
        )
        got = jnp.where(row == r, jnp.take_along_axis(source, lane, axis=1), got)
    permuted[...] = got
    result = front_product(front_ref, lambda c: permuted[c : c + 1, :])
    out_ref[...] = jnp.broadcast_to(result[None], out_ref.shape)


def upper_body(sections, parts_ref, disp_ref, front_ref, out_ref):
    domains = parts_ref.shape[0] // sections
    per_block = parts_ref.shape[2] // LANES

    def row_of(c):
        d, q = c // per_block, (c % per_block) * LANES
        total = parts_ref[d, :, q : q + LANES]
        for s in range(1, sections):
            total = total + parts_ref[s * domains + d, :, q : q + LANES]
        return total

    solved = front_product(front_ref, row_of)
    out_ref[...] = 0.5 * disp_ref[...] + 0.5 * solved


VMEM = pl.BlockSpec(memory_space=pltpu.VMEM)
SMEM = pl.BlockSpec(memory_space=pltpu.SMEM)


def call(body, name, in_specs, out_shape, scratch, cost, limit):
    many = isinstance(out_shape, tuple)
    return pl.pallas_call(
        body,
        out_shape=out_shape,
        in_specs=in_specs,
        out_specs=(VMEM,) * len(out_shape) if many else VMEM,
        scratch_shapes=scratch,
        compiler_params=pltpu.CompilerParams(vmem_limit_bytes=limit),
        cost_estimate=pl.CostEstimate(flops=cost[0], bytes_accessed=cost[1], transcendentals=0),
        name=name,
    )


def f32(*shape):
    return jax.ShapeDtypeStruct(shape, jnp.float32)


def fast_shards(disp_coarse, support_ids, rbf_weights, flow, pivots, lower_inverse, upper_inverse):
    block = disp_coarse.shape[0]
    sections, domains = lax.axis_size("sec"), lax.axis_size("dom")
    chips = domains // 2
    halo = REACH * ITERS
    me = lax.axis_index("dom").astype(jnp.int32).reshape(1)
    ids = support_ids[0, 0]
    weights = jnp.swapaxes(rbf_weights[0, 0], 1, 2)
    field = flow[0]
    count, cells, _ = weights.shape
    comps, _, width = field.shape

    def across(array, k):
        return lax.ppermute(array, "dom", [(i, i ^ (2 * k)) for i in range(domains)])

    def partner(array):
        return lax.ppermute(array, "dom", [(i, i ^ 1) for i in range(domains)])

    def neighbour(array):
        pairs = [(i, (i + 1) % domains if i % 2 else (i - 1) % domains) for i in range(domains)]
        return lax.ppermute(array, "dom", pairs)

    row = disp_coarse.reshape(1, block)
    others = [across(row, k) for k in range(chips - 1, 0, -1)][::-1]
    rows = halo * comps + halo * count * (block // width) + SUB
    near, far, own = call(
        functools.partial(pack_body, halo),
        "pack",
        [SMEM, SMEM, VMEM, VMEM],
        (f32(rows, width), f32(rows, width), f32(SUB, LANES)),
        [],
        (1000, 400_000),
        4 << 20,
    )(me, ids, field, weights)
    far = neighbour(far)
    near = partner(near)
    mine = jnp.concatenate([row] + others, axis=0)
    theirs = partner(mine)

    extent = cells + 2 * halo
    wall, dense = call(
        functools.partial(wall_body, halo),
        "wall",
        [SMEM, SMEM] + [VMEM] * 7,
        (f32(extent, LANES), f32(domains, block)),
        [pltpu.VMEM((comps, extent + 2 * SUB, LANES), jnp.float32)] * 2,
        (4_000_000, 40_000_000),
        8 << 20,
    )(me, ids, mine, theirs, own, near, far, field, weights)

    pair = dense + partner(dense)
    pieces = [pair] + [across(pair, k) for k in range(chips - 1, 0, -1)]
    new_flow = call(
        functools.partial(flow_body, halo),
        "flow",
        [SMEM] + [VMEM] * 4,
        f32(comps, cells, width),
        [pltpu.VMEM((comps, extent + 2 * SUB, width), jnp.float32)] * 2,
        (10_000_000, 4_000_000),
        8 << 20,
    )(me, near, far, field, wall)

    pivot_rows = pivots.reshape(-1, LANES)
    lower = call(
        functools.partial(lower_body, len(pieces)),
        "lower",
        [VMEM] * (len(pieces) + 2),
        f32(sections * domains, 1, block),
        [pltpu.VMEM((domains, block), jnp.float32), pltpu.VMEM(pivot_rows.shape, jnp.float32)],
        (4_000_000, 1_000_000),
        4 << 20,
    )(*pieces, pivot_rows, lower_inverse)
    middle = lax.all_to_all(lower, ("sec", "dom"), 0, 0, tiled=True)
    new_disp = call(
        functools.partial(upper_body, sections),
        "upper",
        [VMEM] * 3,
        f32(1, block),
        [],
        (4_000_000, 1_000_000),
        4 << 20,
    )(middle, row, upper_inverse)
    return (new_flow[None], new_disp.reshape(block))


def fits(mesh):
    chips, odd = divmod(mesh.shape["dom"], 2)
    return odd == 0 and chips & (chips - 1) == 0 and 1 < chips <= 8


def body_for(mesh):
    def body(disp_coarse, support_ids, rbf_weights, flow, pivots, lower_inverse, upper_inverse):
        args = (disp_coarse, support_ids, rbf_weights, flow, pivots, lower_inverse, upper_inverse)
        block = disp_coarse.shape[0]
        cells, width = flow.shape[2:]
        halo = REACH * ITERS
        small = (
            block % width == 0
            and width % LANES == 0
            and cells % 16 == 0
            and halo == SUB
            and support_ids.shape[2] <= SUB
        )
        return fast_shards(*args) if fits(mesh) and small else shards(*args)

    return body


def solution(mesh):
    return jax.shard_map(
        body_for(mesh),
        mesh=mesh,
        in_specs=(
            P("dom"),
            P("sec", "dom", None),
            P("sec", "dom", None, None, None),
            P("sec", None, "dom", None),
            P(),
            P("dom", None),
            P("dom", None),
        ),
        out_specs=(P("sec", None, "dom", None), P("dom")),
        check_vma=False,
    )
```

```python
import functools

import jax
import jax.numpy as jnp
from jax import lax
from jax.experimental import pallas as pl
from jax.experimental.pallas import tpu as pltpu
from jax.sharding import PartitionSpec as P

ITERS = 4
REACH = 2


COURANT = 0.4
MACH = 0.5
DISSIPATION = 0.03125
FACE_AREA = 0.125

LANES = 128
SUB = 8


def padded_2(cells, sides, width):
    for axis, dim in sides:
        count = lax.axis_size(axis)
        head = lax.slice_in_dim(cells, 0, width, axis=dim)
        tail = lax.slice_in_dim(cells, cells.shape[dim] - width, cells.shape[dim], axis=dim)
        cells = jnp.concatenate(
            [
                lax.ppermute(tail, axis, [(i, (i + 1) % count) for i in range(count)]),
                cells,
                lax.ppermute(head, axis, [((i + 1) % count, i) for i in range(count)]),
            ],
            axis=dim,
        )
    return cells


def stencil(padded):
    z_extent = padded.shape[1]
    y_extent = padded.shape[2]
    y_padded = jnp.pad(padded, ((0, 0), (0, 0), (2, 2)))

    def zshift(offset):
        return y_padded[:, 2 + offset : z_extent - 2 + offset, 2 : y_extent + 2]

    def yshift(offset):
        return y_padded[:, 2 : z_extent - 2, 2 + offset : y_extent + 2 + offset]

    centre = zshift(0)
    z_slope = 0.5 * (zshift(1) - zshift(-1))
    y_slope = 0.5 * (yshift(1) - yshift(-1))
    z_fourth = zshift(2) - 4.0 * zshift(1) + 6.0 * centre - 4.0 * zshift(-1) + zshift(-2)
    y_fourth = yshift(2) - 4.0 * yshift(1) + 6.0 * centre - 4.0 * yshift(-1) + yshift(-2)
    damping = DISSIPATION * (z_fourth + y_fourth)
    density = centre[0] - COURANT * (MACH * z_slope[0] + z_slope[2] + y_slope[3]) - damping[0]
    pressure = centre[1] - COURANT * (MACH * z_slope[1] + z_slope[2] + y_slope[3]) - damping[1]
    along = centre[2] - COURANT * (MACH * z_slope[2] + z_slope[1]) - damping[2]
    normal = centre[3] - COURANT * (MACH * z_slope[3] + y_slope[1]) - damping[3]
    return jnp.stack([density, pressure, along, normal])


def with_rims(fields):
    return padded_2(fields, (("dom", 1),), 2)


def shards(disp_coarse, support_ids, rbf_weights, flow, pivots, lower_inverse, upper_inverse):
    block_size = disp_coarse.shape[0]
    domains = lax.axis_size("dom")
    coarse_table = lax.all_gather(
        disp_coarse.astype(jnp.bfloat16), "dom", axis=0, tiled=True
    ).reshape(domains, block_size)
    support = support_ids[0, 0]
    weights = rbf_weights[0, 0]
    matches = support[:, None] == lax.broadcasted_iota(jnp.int32, (support.shape[0], domains), 1)
    choose = matches.astype(jnp.bfloat16)
    picked = jnp.dot(choose, coarse_table, preferred_element_type=jnp.float32).astype(jnp.bfloat16)
    wall_motion = jnp.einsum("kj,kjz->z", picked, weights, preferred_element_type=jnp.float32)
    fields = flow[0].at[3, :, 0].set(wall_motion)
    for sweep_index in range(ITERS):
        fields = stencil(with_rims(fields))
    push = (FACE_AREA * fields[1, :, 0]).astype(jnp.bfloat16)
    terms = jnp.einsum("kjz,z->kj", weights, push, preferred_element_type=jnp.float32)
    dense = jnp.einsum(
        "kb,kj->bj", matches.astype(jnp.float32), terms, precision=lax.Precision.HIGHEST
    )
    owned = lax.psum_scatter(dense, "dom", scatter_dimension=0, tiled=True)
    owned = lax.psum(owned, "sec")
    forces = lax.all_gather(owned, "dom", axis=0, tiled=True).reshape(-1)
    permuted = jnp.take(forces, pivots, axis=0)
    lower_part = jnp.dot(lower_inverse, permuted, precision=lax.Precision.HIGHEST)
    middle = lax.all_gather(lower_part, "dom", axis=0, tiled=True)
    solved = jnp.dot(upper_inverse, middle, precision=lax.Precision.HIGHEST)
    new_disp = 0.5 * disp_coarse + 0.5 * solved
    return (fields[None], new_disp)


def lane_index(shape):
    return lax.broadcasted_iota(jnp.int32, shape, 1)


def sweep(load, lanes, comps):
    shape = load(0, 0).shape
    lane = lane_index(shape)
    width = shape[1]

    def down(f, n):
        return jnp.where(lane >= n, pltpu.roll(f, n, 1), 0.0)

    def up(f, n):
        return jnp.where(lane < width - n, pltpu.roll(f, width - n, 1), 0.0)

    centre = [load(c, 0) for c in range(4)]
    need_y = set(comps) | ({3} if 0 in comps or 1 in comps else set()) | ({1} if 3 in comps else set())
    y_plus = {c: up(centre[c], 1) for c in need_y}
    y_minus = {c: down(centre[c], 1) for c in need_y}
    z_plus = [load(c, 1) for c in range(4)]
    z_minus = [load(c, -1) for c in range(4)]

    def z_slope(c):
        return 0.5 * (z_plus[c] - z_minus[c])

    def y_slope(c):
        return 0.5 * (y_plus[c] - y_minus[c])

    def damping(c):
        near = z_plus[c] + z_minus[c] + y_plus[c] + y_minus[c]
        far = load(c, 2) + load(c, -2) + up(centre[c], 2) + down(centre[c], 2)
        return DISSIPATION * (far - 4.0 * near + 12.0 * centre[c])

    out = {}
    if 0 in comps or 1 in comps:
        spread = z_slope(2) + y_slope(3)
    if 0 in comps:
        out[0] = centre[0] - COURANT * (MACH * z_slope(0) + spread) - damping(0)
    if 1 in comps:
        out[1] = centre[1] - COURANT * (MACH * z_slope(1) + spread) - damping(1)
    if 2 in comps:
        out[2] = centre[2] - COURANT * (MACH * z_slope(2) + z_slope(1)) - damping(2)
    if 3 in comps:
        out[3] = centre[3] - COURANT * (MACH * z_slope(3) + y_slope(1)) - damping(3)
    return out


def pack_body(
    halo, me_ref, ids_hbm, disp_hbm, flow_hbm, wt_hbm,
    near_ref, far_ref, own_ref, row_ref, ids_ref, flow_ref, wt_ref, sem,
):
    odd = me_ref[0] % 2 == 1
    comps, cells, width = flow_hbm.shape
    count = wt_hbm.shape[0]
    halves = wt_hbm.shape[2] // width
    deep = 2 * halo
    copies = [
        (flow_hbm.at[:, pl.ds(0, halo)], flow_ref.at[0]),
        (flow_hbm.at[:, pl.ds(cells - halo, halo)], flow_ref.at[1]),
        (wt_hbm.at[:, pl.ds(0, deep)], wt_ref.at[0]),
        (wt_hbm.at[:, pl.ds(cells - deep, deep)], wt_ref.at[1]),
        (ids_hbm, ids_ref),
        (disp_hbm, row_ref),
    ]
    copies = [pltpu.make_async_copy(src, dst, sem.at[i]) for i, (src, dst) in enumerate(copies)]
    for copy in copies:
        copy.start()
    for copy in copies:
        copy.wait()
    at = 0
    for c in range(comps):
        head, tail = flow_ref[0, c], flow_ref[1, c]
        near_ref[at : at + halo, :] = jnp.where(odd, head, tail)
        far_ref[at : at + halo, :] = jnp.where(odd, tail, head)
        at += halo
    for k in range(count):
        head = wt_ref[0, k].astype(jnp.float32)[0:halo]
        tail = wt_ref[1, k].astype(jnp.float32)[halo:deep]
        near = jnp.where(odd, head, tail)
        far = jnp.where(odd, tail, head)
        for h in range(halves):
            near_ref[at : at + halo, :] = near[:, h * width : (h + 1) * width]
            far_ref[at : at + halo, :] = far[:, h * width : (h + 1) * width]
            at += halo
    row = lax.broadcasted_iota(jnp.int32, (SUB, width), 0)
    ids = jnp.full((SUB, width), -1, jnp.int32)
    for k in range(count):
        ids = jnp.where(row == k, ids_ref[k], ids)
    ids = ids.astype(jnp.float32)
    near_ref[at : at + SUB, :] = ids
    far_ref[at : at + SUB, :] = ids
    own_ref[...] = ids[:, 0:LANES]


def wall_body(
    halo, me_ref, ids_ref, mine_ref, theirs_ref, own_ref, near_ref, far_ref, flow_ref, wt_ref,
    wall_ref, dense_ref, ping, pong,
):
    me = me_ref[0]
    odd = me % 2
    chips = mine_ref.shape[0]
    comps, cells, width = flow_ref.shape
    count, _, block = wt_ref.shape
    halves = block // width
    ids_at = halo * (comps + count * halves)

    slot = lax.broadcasted_iota(jnp.int32, (SUB * 3, 2 * chips), 1)
    chip = (me // 2) ^ (slot % chips)
    core = odd ^ (slot // chips)
    block_of = (2 * chip + core).astype(jnp.float32)
    ids = jnp.concatenate(
        [own_ref[:, 0:1], near_ref[ids_at : ids_at + SUB, 0:1], far_ref[ids_at : ids_at + SUB, 0:1]],
        axis=0,
    )
    choose = (ids == block_of).astype(jnp.bfloat16)
    table = jnp.concatenate([mine_ref[...], theirs_ref[...]], axis=0).astype(jnp.bfloat16)
    picked = jnp.dot(choose, table, preferred_element_type=jnp.float32)

    own = jnp.zeros((cells, LANES), jnp.float32)
    edge = [jnp.zeros((halo, LANES), jnp.float32) for _ in range(2)]
    for k in range(count):
        weights = wt_ref[k].astype(jnp.float32)
        for q in range(0, block, LANES):
            own += weights[:, q : q + LANES] * picked[k : k + 1, q : q + LANES]
            rows = halo * (comps + k * halves + q // width)
            for e, ref in enumerate((near_ref, far_ref)):
                edge[e] += (
                    ref[rows : rows + halo, q % width : q % width + LANES]
                    * picked[SUB * (e + 1) + k : SUB * (e + 1) + k + 1, q : q + LANES]
                )
    own = jnp.sum(own, axis=1, keepdims=True)
    near, far = [jnp.sum(e, axis=1, keepdims=True) for e in edge]
    is_odd = odd == 1
    walls = [
        (SUB, jnp.where(is_odd, near, far)),
        (SUB + halo, own),
        (SUB + halo + cells, jnp.where(is_odd, far, near)),
    ]
    lane = lane_index((1, LANES))
    for at, column in walls:
        rows = column.shape[0]
        column = jnp.broadcast_to(column, (rows, LANES))
        wall_ref[at - SUB : at - SUB + rows, :] = column
        for c in range(comps):
            if rows == cells:
                part = flow_ref[c, :, 0:LANES]
            else:
                a = near_ref[c * halo : (c + 1) * halo, 0:LANES]
                b = far_ref[c * halo : (c + 1) * halo, 0:LANES]
                part = jnp.where(is_odd, a, b) if at == SUB else jnp.where(is_odd, b, a)
            if c == comps - 1:
                part = jnp.where(lane == 0, column, part)
            ping[c, at : at + rows, :] = part

    extent = cells + 2 * halo
    src, dst = ping, pong
    for index in range(ITERS - 1):
        out = sweep(lambda c, o: src[c, SUB + o : SUB + o + extent, :], LANES, (1, 2, 3))
        for c, value in out.items():
            dst[c, SUB : SUB + extent, :] = value
        src, dst = dst, src
    at = SUB + halo
    pressure = sweep(lambda c, o: src[c, at + o : at + o + cells, :], LANES, (1,))[1]
    push = (FACE_AREA * pressure[:, 0:1]).astype(jnp.bfloat16).astype(jnp.float32)
    push = jnp.broadcast_to(push, (cells, LANES))
    dense_ref[...] = jnp.zeros_like(dense_ref)
    for k in range(count):
        weights = wt_ref[k].astype(jnp.float32)
        terms = [
            jnp.sum(weights[:, q : q + LANES] * push, axis=0, keepdims=True)
            for q in range(0, block, LANES)
        ]
        dense_ref[pl.ds(ids_ref[k], 1), :] = jnp.concatenate(terms, axis=1)


def flow_body(halo, me_ref, near_ref, far_ref, flow_ref, wall_ref, out_ref, ping, pong):
    is_odd = me_ref[0] % 2 == 1
    comps, cells, width = flow_ref.shape
    lane = lane_index((1, width))
    for c in range(comps):
        near = near_ref[c * halo : (c + 1) * halo, :]
        far = far_ref[c * halo : (c + 1) * halo, :]
        parts = [
            (0, jnp.where(is_odd, near, far)),
            (halo, flow_ref[c]),
            (halo + cells, jnp.where(is_odd, far, near)),
        ]
        for at, part in parts:
            rows = part.shape[0]
            if c == comps - 1:
                part = jnp.where(lane == 0, wall_ref[at : at + rows, 0:1], part)
            ping[c, SUB + at : SUB + at + rows, :] = part
    src, dst = ping, pong
    extent = cells + 2 * halo
    for index in range(ITERS):
        last = index == ITERS - 1
        first = halo if last else 0
        total = cells if last else extent
        step = 16
        for at in range(first, first + total, step):
            base = SUB + at
            out = sweep(lambda c, o: src[c, base + o : base + o + step, :], width, (0, 1, 2, 3))
            for c, value in out.items():
                if last:
                    out_ref[c, at - halo : at - halo + step, :] = value
                else:
                    dst[c, base : base + step, :] = value
        src, dst = dst, src


def spread_rows(columns, row_of):
    return [jnp.broadcast_to(row_of(c), (SUB, LANES)) for c in range(columns // LANES)]


def front_product(front_ref, spread):
    rows, columns = front_ref.shape
    out = []
    for top in range(0, rows, LANES):
        parts = []
        for at in range(top, top + LANES, SUB):
            total = None
            for c in range(columns // LANES):
                term = front_ref[at : at + SUB, c * LANES : (c + 1) * LANES] * spread[c]
                total = term if total is None else total + term
            parts.append(total)
        out.append(jnp.sum(jnp.concatenate(parts, axis=0).T, axis=0, keepdims=True))
    return jnp.concatenate(out, axis=1)


def lower_body(parts, *refs):
    pieces = refs[:parts]
    pivots_ref, front_ref, out_ref, table, permuted = refs[parts:]
    total = pieces[0][...]
    for ref in pieces[1:]:
        total = total + ref[...]
    table[...] = total
    block = table.shape[1]
    per_block = block // LANES
    pivot = pivots_ref[...]
    shift = LANES.bit_length() - 1
    row = jnp.right_shift(pivot, shift)
    lane = jnp.bitwise_and(pivot, LANES - 1)
    got = jnp.zeros(pivot.shape, jnp.float32)
    for r in range(pivot.shape[0]):
        q = (r % per_block) * LANES
        source = jnp.broadcast_to(
            table[r // per_block : r // per_block + 1, q : q + LANES], pivot.shape
        )
        got = jnp.where(row == r, jnp.take_along_axis(source, lane, axis=1), got)
    permuted[...] = got
    spread = spread_rows(front_ref.shape[1], lambda c: permuted[c : c + 1, :])
    result = front_product(front_ref, spread)
    out_ref[...] = jnp.broadcast_to(result[None], out_ref.shape)


def upper_body(sections, stages, parts_ref, disp_hbm, front_hbm, out_ref, disp_ref, front_ref, sem):
    rows = front_hbm.shape[0] // stages
    copies = [
        pltpu.make_async_copy(
            front_hbm.at[pl.ds(i * rows, rows)], front_ref.at[pl.ds(i * rows, rows)], sem.at[i]
        )
        for i in range(stages)
    ]
    copies.append(pltpu.make_async_copy(disp_hbm, disp_ref, sem.at[stages]))
    for copy in copies:
        copy.start()
    domains = parts_ref.shape[0] // sections
    per_block = parts_ref.shape[2] // LANES

    def row_of(c):
        d, q = c // per_block, (c % per_block) * LANES
        total = parts_ref[d, :, q : q + LANES]
        for s in range(1, sections):
            total = total + parts_ref[s * domains + d, :, q : q + LANES]
        return total

    spread = spread_rows(front_hbm.shape[1], row_of)
    solved = []
    for i in range(stages):
        copies[i].wait()
        solved.append(front_product(front_ref.at[pl.ds(i * rows, rows)], spread))
    copies[stages].wait()
    out_ref[...] = 0.5 * disp_ref[...] + 0.5 * jnp.concatenate(solved, axis=1)


VMEM = pl.BlockSpec(memory_space=pltpu.VMEM)
SMEM = pl.BlockSpec(memory_space=pltpu.SMEM)
HBM = pl.BlockSpec(memory_space=pltpu.HBM)

COVER = 20_000_000_000


def call(body, name, in_specs, out_shape, scratch, cost, limit):
    many = isinstance(out_shape, tuple)
    return pl.pallas_call(
        body,
        out_shape=out_shape,
        in_specs=in_specs,
        out_specs=(VMEM,) * len(out_shape) if many else VMEM,
        scratch_shapes=scratch,
        compiler_params=pltpu.CompilerParams(vmem_limit_bytes=limit),
        cost_estimate=pl.CostEstimate(flops=cost[0], bytes_accessed=cost[1], transcendentals=0),
        name=name,
    )


def in_hbm(array):
    return pltpu.with_memory_space_constraint(array, pltpu.HBM)


def f32(*shape):
    return jax.ShapeDtypeStruct(shape, jnp.float32)


def fast_shards(disp_coarse, support_ids, rbf_weights, flow, pivots, lower_inverse, upper_inverse):
    block = disp_coarse.shape[0]
    sections, domains = lax.axis_size("sec"), lax.axis_size("dom")
    chips = domains // 2
    halo = REACH * ITERS
    me = lax.axis_index("dom").astype(jnp.int32).reshape(1)
    ids = support_ids[0, 0]
    weights = jnp.swapaxes(rbf_weights[0, 0], 1, 2)
    field = flow[0]
    count, cells, _ = weights.shape
    comps, _, width = field.shape

    def across(array, k):
        return lax.ppermute(array, "dom", [(i, i ^ (2 * k)) for i in range(domains)])

    def partner(array):
        return lax.ppermute(array, "dom", [(i, i ^ 1) for i in range(domains)])

    def neighbour(array):
        pairs = [(i, (i + 1) % domains if i % 2 else (i - 1) % domains) for i in range(domains)]
        return lax.ppermute(array, "dom", pairs)

    row = disp_coarse.reshape(1, block)
    others = [across(row, k) for k in range(chips - 1, 0, -1)][::-1]
    rows = halo * comps + halo * count * (block // width) + SUB
    near, far, own, mine = call(
        functools.partial(pack_body, halo),
        "pack",
        [SMEM] + [HBM] * 4,
        (f32(rows, width), f32(rows, width), f32(SUB, LANES), f32(1, block)),
        [
            pltpu.SMEM((count,), jnp.int32),
            pltpu.VMEM((2, comps, halo, width), jnp.float32),
            pltpu.VMEM((2, count, 2 * halo, block), weights.dtype),
            pltpu.SemaphoreType.DMA((6,)),
        ],
        (COVER, 400_000),
        4 << 20,
    )(me, *[in_hbm(x) for x in (ids, row, field, weights)])
    far = neighbour(far)
    near = partner(near)
    mine = jnp.concatenate([mine] + others, axis=0)
    theirs = partner(mine)

    extent = cells + 2 * halo
    wall, dense = call(
        functools.partial(wall_body, halo),
        "wall",
        [SMEM, SMEM] + [VMEM] * 7,
        (f32(extent, LANES), f32(domains, block)),
        [pltpu.VMEM((comps, extent + 2 * SUB, LANES), jnp.float32)] * 2,
        (COVER, 40_000_000),
        8 << 20,
    )(me, ids, mine, theirs, own, near, far, field, weights)

    pair = dense + partner(dense)
    pieces = [pair] + [across(pair, k) for k in range(chips - 1, 0, -1)]
    new_flow = call(
        functools.partial(flow_body, halo),
        "flow",
        [SMEM] + [VMEM] * 4,
        f32(comps, cells, width),
        [pltpu.VMEM((comps, extent + 2 * SUB, width), jnp.float32)] * 2,
        (COVER, 4_000_000),
        8 << 20,
    )(me, near, far, field, wall)

    pivot_rows = pivots.reshape(-1, LANES)
    lower = call(
        functools.partial(lower_body, len(pieces)),
        "lower",
        [VMEM] * (len(pieces) + 2),
        f32(sections * domains, 1, block),
        [pltpu.VMEM((domains, block), jnp.float32), pltpu.VMEM(pivot_rows.shape, jnp.float32)],
        (COVER, 1_000_000),
        4 << 20,
    )(*pieces, pivot_rows, lower_inverse)
    middle = lax.all_to_all(lower, ("sec", "dom"), 0, 0, tiled=True)
    stages = block // LANES
    new_disp = call(
        functools.partial(upper_body, sections, stages),
        "upper",
        [VMEM, HBM, HBM],
        f32(1, block),
        [
            pltpu.VMEM((1, block), jnp.float32),
            pltpu.VMEM(upper_inverse.shape, jnp.float32),
            pltpu.SemaphoreType.DMA((stages + 1,)),
        ],
        (COVER, 1_000_000),
        12 << 20,
    )(middle, in_hbm(row), in_hbm(upper_inverse))
    return (new_flow[None], new_disp.reshape(block))


def fits(mesh):
    chips, odd = divmod(mesh.shape["dom"], 2)
    return odd == 0 and chips & (chips - 1) == 0 and 1 < chips <= 8


def body_for(mesh):
    def body(disp_coarse, support_ids, rbf_weights, flow, pivots, lower_inverse, upper_inverse):
        args = (disp_coarse, support_ids, rbf_weights, flow, pivots, lower_inverse, upper_inverse)
        block = disp_coarse.shape[0]
        cells, width = flow.shape[2:]
        halo = REACH * ITERS
        small = (
            block % width == 0
            and width % LANES == 0
            and cells % (4 * halo) == 0
            and halo == SUB
            and support_ids.shape[2] <= SUB
        )
        return fast_shards(*args) if fits(mesh) and small else shards(*args)

    return body


def solution(mesh):
    return jax.shard_map(
        body_for(mesh),
        mesh=mesh,
        in_specs=(
            P("dom"),
            P("sec", "dom", None),
            P("sec", "dom", None, None, None),
            P("sec", None, "dom", None),
            P(),
            P("dom", None),
            P("dom", None),
        ),
        out_specs=(P("sec", None, "dom", None), P("dom")),
        check_vma=False,
    )
```

```python
import functools

import jax
import jax.numpy as jnp
from jax import lax
from jax.experimental import pallas as pl
from jax.experimental.pallas import tpu as pltpu
from jax.sharding import PartitionSpec as P


ITERS = 4
REACH = 2


COURANT = 0.4
MACH = 0.5
DISSIPATION = 0.03125
FACE_AREA = 0.125

LANES = 128
SUB = 8
GROUP = LANES // 4


def padded_2(cells, sides, width):
    for axis, dim in sides:
        count = lax.axis_size(axis)
        head = lax.slice_in_dim(cells, 0, width, axis=dim)
        tail = lax.slice_in_dim(cells, cells.shape[dim] - width, cells.shape[dim], axis=dim)
        cells = jnp.concatenate(
            [
                lax.ppermute(tail, axis, [(i, (i + 1) % count) for i in range(count)]),
                cells,
                lax.ppermute(head, axis, [((i + 1) % count, i) for i in range(count)]),
            ],
            axis=dim,
        )
    return cells


def stencil(padded):
    z_extent = padded.shape[1]
    y_extent = padded.shape[2]
    y_padded = jnp.pad(padded, ((0, 0), (0, 0), (2, 2)))

    def zshift(offset):
        return y_padded[:, 2 + offset : z_extent - 2 + offset, 2 : y_extent + 2]

    def yshift(offset):
        return y_padded[:, 2 : z_extent - 2, 2 + offset : y_extent + 2 + offset]

    centre = zshift(0)
    z_slope = 0.5 * (zshift(1) - zshift(-1))
    y_slope = 0.5 * (yshift(1) - yshift(-1))
    z_fourth = zshift(2) - 4.0 * zshift(1) + 6.0 * centre - 4.0 * zshift(-1) + zshift(-2)
    y_fourth = yshift(2) - 4.0 * yshift(1) + 6.0 * centre - 4.0 * yshift(-1) + yshift(-2)
    damping = DISSIPATION * (z_fourth + y_fourth)
    density = centre[0] - COURANT * (MACH * z_slope[0] + z_slope[2] + y_slope[3]) - damping[0]
    pressure = centre[1] - COURANT * (MACH * z_slope[1] + z_slope[2] + y_slope[3]) - damping[1]
    along = centre[2] - COURANT * (MACH * z_slope[2] + z_slope[1]) - damping[2]
    normal = centre[3] - COURANT * (MACH * z_slope[3] + y_slope[1]) - damping[3]
    return jnp.stack([density, pressure, along, normal])


def with_rims(fields):
    return padded_2(fields, (("dom", 1),), 2)


def shards(disp_coarse, support_ids, rbf_weights, flow, pivots, lower_inverse, upper_inverse):
    block_size = disp_coarse.shape[0]
    domains = lax.axis_size("dom")
    coarse_table = lax.all_gather(
        disp_coarse.astype(jnp.bfloat16), "dom", axis=0, tiled=True
    ).reshape(domains, block_size)
    support = support_ids[0, 0]
    weights = rbf_weights[0, 0]
    matches = support[:, None] == lax.broadcasted_iota(jnp.int32, (support.shape[0], domains), 1)
    choose = matches.astype(jnp.bfloat16)
    picked = jnp.dot(choose, coarse_table, preferred_element_type=jnp.float32).astype(jnp.bfloat16)
    wall_motion = jnp.einsum("kj,kjz->z", picked, weights, preferred_element_type=jnp.float32)
    fields = flow[0].at[3, :, 0].set(wall_motion)
    for _ in range(ITERS):
        fields = stencil(with_rims(fields))
    push = (FACE_AREA * fields[1, :, 0]).astype(jnp.bfloat16)
    terms = jnp.einsum("kjz,z->kj", weights, push, preferred_element_type=jnp.float32)
    dense = jnp.einsum(
        "kb,kj->bj", matches.astype(jnp.float32), terms, precision=lax.Precision.HIGHEST
    )
    owned = lax.psum_scatter(dense, "dom", scatter_dimension=0, tiled=True)
    owned = lax.psum(owned, "sec")
    forces = lax.all_gather(owned, "dom", axis=0, tiled=True).reshape(-1)
    permuted = jnp.take(forces, pivots, axis=0)
    lower_part = jnp.dot(lower_inverse, permuted, precision=lax.Precision.HIGHEST)
    middle = lax.all_gather(lower_part, "dom", axis=0, tiled=True)
    solved = jnp.dot(upper_inverse, middle, precision=lax.Precision.HIGHEST)
    new_disp = 0.5 * disp_coarse + 0.5 * solved
    return (fields[None], new_disp)


def lane_index(shape):
    return lax.broadcasted_iota(jnp.int32, shape, 1)


def sweep(load, comps):
    shape = load(0, 0).shape
    lane = lane_index(shape)
    width = shape[1]

    def down(f, n):
        return jnp.where(lane >= n, pltpu.roll(f, n, 1), 0.0)

    def up(f, n):
        return jnp.where(lane < width - n, pltpu.roll(f, width - n, 1), 0.0)

    centre = [load(c, 0) for c in range(4)]
    need_y = set(comps) | ({3} if 0 in comps or 1 in comps else set()) | ({1} if 3 in comps else set())
    y_plus = {c: up(centre[c], 1) for c in need_y}
    y_minus = {c: down(centre[c], 1) for c in need_y}
    z_plus = [load(c, 1) for c in range(4)]
    z_minus = [load(c, -1) for c in range(4)]

    def z_slope(c):
        return 0.5 * (z_plus[c] - z_minus[c])

    def y_slope(c):
        return 0.5 * (y_plus[c] - y_minus[c])

    def damping(c):
        near = z_plus[c] + z_minus[c] + y_plus[c] + y_minus[c]
        far = load(c, 2) + load(c, -2) + up(centre[c], 2) + down(centre[c], 2)
        return DISSIPATION * (far - 4.0 * near + 12.0 * centre[c])

    out = {}
    if 0 in comps or 1 in comps:
        spread = z_slope(2) + y_slope(3)
    if 0 in comps:
        out[0] = centre[0] - COURANT * (MACH * z_slope(0) + spread) - damping(0)
    if 1 in comps:
        out[1] = centre[1] - COURANT * (MACH * z_slope(1) + spread) - damping(1)
    if 2 in comps:
        out[2] = centre[2] - COURANT * (MACH * z_slope(2) + z_slope(1)) - damping(2)
    if 3 in comps:
        out[3] = centre[3] - COURANT * (MACH * z_slope(3) + y_slope(1)) - damping(3)
    return out


def pack_body(
    halo, me_ref, ids_hbm, disp_hbm, flow_hbm, wt_hbm,
    near_ref, far_ref, own_ref, row_ref, ids_ref, flow_ref, wt_ref, sem,
):
    odd = me_ref[0] % 2 == 1
    comps, cells, width = flow_hbm.shape
    count = wt_hbm.shape[0]
    halves = wt_hbm.shape[2] // width
    deep = 2 * halo
    copies = [
        (flow_hbm.at[:, pl.ds(0, halo)], flow_ref.at[0]),
        (flow_hbm.at[:, pl.ds(cells - halo, halo)], flow_ref.at[1]),
        (wt_hbm.at[:, pl.ds(0, deep)], wt_ref.at[0]),
        (wt_hbm.at[:, pl.ds(cells - deep, deep)], wt_ref.at[1]),
        (ids_hbm, ids_ref),
        (disp_hbm, row_ref),
    ]
    copies = [pltpu.make_async_copy(src, dst, sem.at[i]) for i, (src, dst) in enumerate(copies)]
    for copy in copies:
        copy.start()
    for copy in copies:
        copy.wait()
    at = 0
    for c in range(comps):
        head, tail = flow_ref[0, c], flow_ref[1, c]
        near_ref[at : at + halo, :] = jnp.where(odd, head, tail)
        far_ref[at : at + halo, :] = jnp.where(odd, tail, head)
        at += halo
    for k in range(count):
        head = wt_ref[0, k].astype(jnp.float32)[0:halo]
        tail = wt_ref[1, k].astype(jnp.float32)[halo:deep]
        near = jnp.where(odd, head, tail)
        far = jnp.where(odd, tail, head)
        for h in range(halves):
            near_ref[at : at + halo, :] = near[:, h * width : (h + 1) * width]
            far_ref[at : at + halo, :] = far[:, h * width : (h + 1) * width]
            at += halo
    row = lax.broadcasted_iota(jnp.int32, (SUB, width), 0)
    ids = jnp.full((SUB, width), -1, jnp.int32)
    for k in range(count):
        ids = jnp.where(row == k, ids_ref[k], ids)
    ids = ids.astype(jnp.float32)
    near_ref[at : at + SUB, :] = ids
    far_ref[at : at + SUB, :] = ids
    own_ref[...] = ids[:, 0:LANES]


def wall_body(
    halo, me_ref, ids_ref, mine_ref, theirs_ref, own_ref, near_ref, far_ref, flow_ref, wt_ref, pivots_ref,
    wall_ref, permuted_ref, ping, pong,
):
    me = me_ref[0]
    odd = me % 2
    is_odd = odd == 1
    chips = mine_ref.shape[0]
    comps, cells, width = flow_ref.shape
    count, _, block = wt_ref.shape
    halves = block // width
    ids_at = halo * (comps + count * halves)

    slot = lax.broadcasted_iota(jnp.int32, (SUB * 3, 2 * chips), 1)
    chip = (me // 2) ^ (slot % chips)
    core = odd ^ (slot // chips)
    block_of = (2 * chip + core).astype(jnp.float32)
    ids = jnp.concatenate(
        [own_ref[:, 0:1], near_ref[ids_at : ids_at + SUB, 0:1], far_ref[ids_at : ids_at + SUB, 0:1]],
        axis=0,
    )
    choose = (ids == block_of).astype(jnp.bfloat16)
    table = jnp.concatenate([mine_ref[...], theirs_ref[...]], axis=0).astype(jnp.bfloat16)
    picked = jnp.dot(choose, table, preferred_element_type=jnp.float32)

    own = jnp.zeros((cells, LANES), jnp.float32)
    edge = [jnp.zeros((halo, LANES), jnp.float32) for _ in range(2)]
    for k in range(count):
        weights = wt_ref[k].astype(jnp.float32)
        for q in range(0, block, LANES):
            own += weights[:, q : q + LANES] * picked[k : k + 1, q : q + LANES]
            rows = halo * (comps + k * halves + q // width)
            for e, ref in enumerate((near_ref, far_ref)):
                edge[e] += (
                    ref[rows : rows + halo, q % width : q % width + LANES]
                    * picked[SUB * (e + 1) + k : SUB * (e + 1) + k + 1, q : q + LANES]
                )
    own = jnp.sum(own, axis=1, keepdims=True)
    near, far = [jnp.sum(e, axis=1, keepdims=True) for e in edge]

    def beside(load):
        group = lane_index((1, LANES)) // GROUP
        pressure, along, normal = [load(c)[:, 0:LANES] for c in (1, 2, 3)]
        packed = jnp.where(group == 1, pltpu.roll(along, GROUP, 1), pressure)
        return jnp.where(group == 2, pltpu.roll(normal, 2 * GROUP, 1), packed)

    at_near, at_far = [
        beside(lambda c: ref[c * halo : (c + 1) * halo, :]) for ref in (near_ref, far_ref)
    ]
    first = lane_index((1, LANES)) == 2 * GROUP
    parts = [
        (0, jnp.where(is_odd, near, far), jnp.where(is_odd, at_near, at_far)),
        (halo, own, beside(lambda c: flow_ref[c])),
        (halo + cells, jnp.where(is_odd, far, near), jnp.where(is_odd, at_far, at_near)),
    ]
    for at, column, part in parts:
        rows = column.shape[0]
        column = jnp.broadcast_to(column, (rows, LANES))
        wall_ref[at : at + rows, :] = column
        ping[SUB + at : SUB + at + rows, :] = jnp.where(first, column, part)

    extent = cells + 2 * halo
    src, dst = ping, pong
    for index in range(ITERS):
        at, rows = (SUB, extent) if index < ITERS - 1 else (SUB + halo, cells)
        lane = lane_index((rows, LANES))
        group = lane // GROUP
        height = lane % GROUP
        centre = src[at : at + rows, :]
        z_plus, z_minus = [src[at + o : at + o + rows, :] for o in (1, -1)]
        y_plus = pltpu.roll(centre, LANES - 1, 1)
        y_minus = jnp.where(height >= 1, pltpu.roll(centre, 1, 1), 0.0)
        far_y = pltpu.roll(centre, LANES - 2, 1) + jnp.where(height >= 2, pltpu.roll(centre, 2, 1), 0.0)
        far_z = src[at + 2 : at + 2 + rows, :] + src[at - 2 : at - 2 + rows, :]
        damping = DISSIPATION * (
            far_y + far_z - 4.0 * (z_plus + z_minus + y_plus + y_minus) + 12.0 * centre
        )
        z_slope = 0.5 * (z_plus - z_minus)
        other_y = 0.5 * (
            pltpu.roll(centre, 2 * GROUP - 1, 1)
            - jnp.where(height >= 1, pltpu.roll(centre, 2 * GROUP + 1, 1), 0.0)
        )
        cross = jnp.where(group == 0, pltpu.roll(z_slope, LANES - GROUP, 1) + other_y, other_y)
        cross = jnp.where(group == 1, pltpu.roll(z_slope, GROUP, 1), cross)
        value = centre - COURANT * (MACH * z_slope + cross) - damping
        if index < ITERS - 1:
            dst[at : at + rows, :] = jnp.where(group == 3, 0.0, value)
        src, dst = dst, src
    push = (FACE_AREA * value[:, 0:1]).astype(jnp.bfloat16).astype(jnp.float32)
    push = jnp.broadcast_to(push, (cells, LANES))

    pivot = pivots_ref[...]
    row = jnp.right_shift(pivot, LANES.bit_length() - 1)
    lane = jnp.bitwise_and(pivot, LANES - 1)
    got = jnp.zeros(pivot.shape, jnp.float32)
    for k in range(count):
        weights = wt_ref[k].astype(jnp.float32)
        for q in range(block // LANES):
            term = jnp.sum(weights[:, q * LANES : (q + 1) * LANES] * push, axis=0, keepdims=True)
            source = jnp.take_along_axis(jnp.broadcast_to(term, pivot.shape), lane, axis=1)
            got = jnp.where(row == ids_ref[k] * (block // LANES) + q, source, got)
    permuted_ref[...] = got


def flow_body(
    halo, me_ref, near_ref, far_ref, flow_hbm, wall_ref, front_hbm, out_ref, tail_ref, ping, pong, sem
):
    left = front_hbm.shape[1] - tail_ref.shape[1]
    fetch = pltpu.make_async_copy(front_hbm.at[:, pl.ds(left, tail_ref.shape[1])], tail_ref, sem.at[0])
    fetch.start()
    is_odd = me_ref[0] % 2 == 1
    comps, cells, width = flow_hbm.shape
    middle = SUB + halo
    field = pltpu.make_async_copy(flow_hbm, ping.at[:, pl.ds(middle, cells)], sem.at[1])
    field.start()
    lane = lane_index((1, width))
    for c in range(comps):
        near = near_ref[c * halo : (c + 1) * halo, :]
        far = far_ref[c * halo : (c + 1) * halo, :]
        for at, part in ((0, jnp.where(is_odd, near, far)), (halo + cells, jnp.where(is_odd, far, near))):
            if c == comps - 1:
                part = jnp.where(lane == 0, wall_ref[at : at + halo, 0:1], part)
            ping[c, SUB + at : SUB + at + halo, :] = part
    field.wait()
    wall = wall_ref[halo : halo + cells, :]
    normal = ping[comps - 1, middle : middle + cells, 0:LANES]
    ping[comps - 1, middle : middle + cells, 0:LANES] = jnp.where(lane_index((1, LANES)) == 0, wall, normal)
    src, dst = ping, pong
    extent = cells + 2 * halo
    for index in range(ITERS):
        last = index == ITERS - 1
        first = halo if last else 0
        total = cells if last else extent
        step = 16
        for at in range(first, first + total, step):
            base = SUB + at
            out = sweep(lambda c, o: src[c, base + o : base + o + step, :], (0, 1, 2, 3))
            for c, value in out.items():
                if last:
                    out_ref[c, at - halo : at - halo + step, :] = value
                else:
                    dst[c, base : base + step, :] = value
        src, dst = dst, src
    fetch.wait()


def spread_rows(columns, row_of):
    return [jnp.broadcast_to(row_of(c), (SUB, LANES)) for c in range(columns // LANES)]


def front_product(front_ref, spread):
    rows, columns = front_ref.shape
    out = []
    for top in range(0, rows, LANES):
        parts = []
        for at in range(top, top + LANES, SUB):
            total = None
            for c in range(columns // LANES):
                term = front_ref[at : at + SUB, c * LANES : (c + 1) * LANES] * spread[c]
                total = term if total is None else total + term
            parts.append(total)
        out.append(jnp.sum(jnp.concatenate(parts, axis=0).T, axis=0, keepdims=True))
    return jnp.concatenate(out, axis=1)


def lower_body(parts, *refs):
    front_ref, out_ref, permuted = refs[parts:]
    total = refs[0][...]
    for ref in refs[1:parts]:
        total = total + ref[...]
    permuted[...] = total
    spread = spread_rows(front_ref.shape[1], lambda c: permuted[c : c + 1, :])
    result = front_product(front_ref, spread)
    out_ref[...] = jnp.broadcast_to(result[None], out_ref.shape)


def upper_body(
    sections, me_ref, parts_ref, disp_hbm, tail_ref, front_hbm, out_ref, disp_ref, head_ref, total, sem
):
    me = me_ref[0]
    block = parts_ref.shape[2]
    domains = parts_ref.shape[0] // sections
    heads = head_ref.shape[0]
    copies = [
        pltpu.make_async_copy(
            front_hbm.at[:, pl.ds(b * block, block)], head_ref.at[b], sem.at[b]
        )
        for b in range(heads)
    ]
    own = pltpu.make_async_copy(disp_hbm, disp_ref, sem.at[heads])
    own.start()
    for b in reversed(range(heads)):
        pl.when(b >= me)(copies[b].start)
    total[...] = jnp.zeros_like(total)
    for b in reversed(range(domains)):

        def add(b=b):
            if b < heads:
                copies[b].wait()
            rows = []
            for q in range(0, block, LANES):
                first = (domains - 1 - b) * sections
                part = parts_ref[first, :, q : q + LANES]
                for s in range(1, sections):
                    part = part + parts_ref[first + s, :, q : q + LANES]
                rows.append(jnp.broadcast_to(part, (SUB, LANES)))
            for at in range(0, block, SUB):
                value = total[at : at + SUB, :]
                for i, row in enumerate(rows):
                    if b < heads:
                        front = head_ref[b, at : at + SUB, i * LANES : (i + 1) * LANES]
                    else:
                        left = (b - heads) * block + i * LANES
                        front = tail_ref[at : at + SUB, left : left + LANES]
                    value = value + front * row
                total[at : at + SUB, :] = value

        pl.when(b >= me)(add)
    solved = [
        jnp.sum(total[at : at + LANES, :].T, axis=0, keepdims=True) for at in range(0, block, LANES)
    ]
    own.wait()
    out_ref[...] = 0.5 * disp_ref[...] + 0.5 * jnp.concatenate(solved, axis=1)


VMEM = pl.BlockSpec(memory_space=pltpu.VMEM)
SMEM = pl.BlockSpec(memory_space=pltpu.SMEM)
HBM = pl.BlockSpec(memory_space=pltpu.HBM)

COVER = 20_000_000_000

TAIL_BYTES = 2 << 20


def call(body, in_specs, out_shape, scratch, cost, limit):
    many = isinstance(out_shape, tuple)
    return pl.pallas_call(
        body,
        out_shape=out_shape,
        in_specs=in_specs,
        out_specs=(VMEM,) * len(out_shape) if many else VMEM,
        scratch_shapes=scratch,
        compiler_params=pltpu.CompilerParams(vmem_limit_bytes=limit),
        cost_estimate=pl.CostEstimate(flops=cost[0], bytes_accessed=cost[1], transcendentals=0),
    )


def in_hbm(array):
    return pltpu.with_memory_space_constraint(array, pltpu.HBM)


def f32(*shape):
    return jax.ShapeDtypeStruct(shape, jnp.float32)


def fast_shards(disp_coarse, support_ids, rbf_weights, flow, pivots, lower_inverse, upper_inverse):
    block = disp_coarse.shape[0]
    sections, domains = lax.axis_size("sec"), lax.axis_size("dom")
    chips = domains // 2
    halo = REACH * ITERS
    me = lax.axis_index("dom").astype(jnp.int32).reshape(1)
    ids = support_ids[0, 0]
    weights = jnp.swapaxes(rbf_weights[0, 0], 1, 2)
    field = flow[0]
    count, cells, _ = weights.shape
    comps, _, width = field.shape

    def across(array, k):
        return lax.ppermute(array, "dom", [(i, i ^ (2 * k)) for i in range(domains)])

    def partner(array):
        return lax.ppermute(array, "dom", [(i, i ^ 1) for i in range(domains)])

    def neighbour(array):
        pairs = [(i, (i + 1) % domains if i % 2 else (i - 1) % domains) for i in range(domains)]
        return lax.ppermute(array, "dom", pairs)

    row = disp_coarse.reshape(1, block)
    rows = halo * comps + halo * count * (block // width) + SUB
    near, far, own, mine = call(
        functools.partial(pack_body, halo),
        [SMEM] + [HBM] * 4,
        (f32(rows, width), f32(rows, width), f32(SUB, LANES), f32(1, block)),
        [
            pltpu.SMEM((count,), jnp.int32),
            pltpu.VMEM((2, comps, halo, width), jnp.float32),
            pltpu.VMEM((2, count, 2 * halo, block), weights.dtype),
            pltpu.SemaphoreType.DMA((6,)),
        ],
        (COVER, 400_000),
        4 << 20,
    )(me, *[in_hbm(x) for x in (ids, row, field, weights)])
    far = neighbour(far)
    near = partner(near)
    others = []
    for k in range(1, chips):
        others.append(across(row if k == chips - 1 else mine, k))
    mine = jnp.concatenate([mine] + others, axis=0)
    theirs = partner(mine)

    extent = cells + 2 * halo
    pivot_rows = pivots.reshape(-1, LANES)
    wall, permuted = call(
        functools.partial(wall_body, halo),
        [SMEM, SMEM] + [VMEM] * 8,
        (f32(extent, LANES), f32(*pivot_rows.shape)),
        [pltpu.VMEM((extent + 2 * SUB, LANES), jnp.float32)] * 2,
        (COVER, 40_000_000),
        8 << 20,
    )(me, ids, mine, theirs, own, near, far, field, weights, pivot_rows)

    pair = permuted + partner(permuted)
    pieces = [pair] + [across(pair, k) for k in range(chips - 1, 0, -1)]
    tails = max(1, min(domains - 1, TAIL_BYTES // (4 * block * block)))
    new_flow, tail = call(
        functools.partial(flow_body, halo),
        [SMEM, VMEM, VMEM, HBM, VMEM, HBM],
        (f32(comps, cells, width), f32(block, tails * block)),
        [pltpu.VMEM((comps, extent + 2 * SUB, width), jnp.float32)] * 2
        + [pltpu.SemaphoreType.DMA((2,))],
        (COVER, 4_000_000),
        8 << 20,
    )(me, near, far, in_hbm(field), wall, in_hbm(upper_inverse))

    lower = call(
        functools.partial(lower_body, len(pieces)),
        [VMEM] * (len(pieces) + 1),
        f32(sections * domains, 1, block),
        [pltpu.VMEM(pivot_rows.shape, jnp.float32)],
        (COVER, 1_000_000),
        4 << 20,
    )(*pieces, lower_inverse)
    order = [s * domains + d for d in reversed(range(domains)) for s in range(sections)]
    middle = lax.all_to_all(
        lower, ("sec", "dom"), 0, 0, axis_index_groups=[order], tiled=True
    )
    new_disp = call(
        functools.partial(upper_body, sections),
        [SMEM, VMEM, HBM, VMEM, HBM],
        f32(1, block),
        [
            pltpu.VMEM((1, block), jnp.float32),
            pltpu.VMEM((domains - tails, block, block), jnp.float32),
            pltpu.VMEM((block, LANES), jnp.float32),
            pltpu.SemaphoreType.DMA((domains - tails + 1,)),
        ],
        (COVER, 1_000_000),
        12 << 20,
    )(me, middle, in_hbm(row), tail, in_hbm(upper_inverse))
    return (new_flow[None], new_disp.reshape(block))


def fits(mesh):
    chips, odd = divmod(mesh.shape["dom"], 2)
    return odd == 0 and chips & (chips - 1) == 0 and 1 < chips <= 8


def body_for(mesh):
    def body(disp_coarse, support_ids, rbf_weights, flow, pivots, lower_inverse, upper_inverse):
        args = (disp_coarse, support_ids, rbf_weights, flow, pivots, lower_inverse, upper_inverse)
        block = disp_coarse.shape[0]
        cells, width = flow.shape[2:]
        halo = REACH * ITERS
        small = (
            block % width == 0
            and width % LANES == 0
            and cells % (4 * halo) == 0
            and halo == SUB
            and 2 * halo < GROUP
            and flow.shape[1] == 4
            and pivots.shape[0] % (SUB * LANES) == 0
            and support_ids.shape[2] <= SUB
        )
        return fast_shards(*args) if fits(mesh) and small else shards(*args)

    return body


def solution(mesh):
    return jax.shard_map(
        body_for(mesh),
        mesh=mesh,
        in_specs=(
            P("dom"),
            P("sec", "dom", None),
            P("sec", "dom", None, None, None),
            P("sec", None, "dom", None),
            P(),
            P("dom", None),
            P("dom", None),
        ),
        out_specs=(P("sec", None, "dom", None), P("dom")),
        check_vma=False,
    )
```

```python
import functools

import jax
import jax.numpy as jnp
from jax import lax
from jax.experimental import pallas as pl
from jax.experimental.pallas import tpu as pltpu
from jax.sharding import PartitionSpec as P


ITERS = 4
REACH = 2


COURANT = 0.4
MACH = 0.5
DISSIPATION = 0.03125
FACE_AREA = 0.125

LANES = 128
SUB = 8
GROUP = LANES // 4


def padded_2(cells, sides, width):
    for axis, dim in sides:
        count = lax.axis_size(axis)
        head = lax.slice_in_dim(cells, 0, width, axis=dim)
        tail = lax.slice_in_dim(cells, cells.shape[dim] - width, cells.shape[dim], axis=dim)
        cells = jnp.concatenate(
            [
                lax.ppermute(tail, axis, [(i, (i + 1) % count) for i in range(count)]),
                cells,
                lax.ppermute(head, axis, [((i + 1) % count, i) for i in range(count)]),
            ],
            axis=dim,
        )
    return cells


def stencil(padded):
    z_extent = padded.shape[1]
    y_extent = padded.shape[2]
    y_padded = jnp.pad(padded, ((0, 0), (0, 0), (2, 2)))

    def zshift(offset):
        return y_padded[:, 2 + offset : z_extent - 2 + offset, 2 : y_extent + 2]

    def yshift(offset):
        return y_padded[:, 2 : z_extent - 2, 2 + offset : y_extent + 2 + offset]

    centre = zshift(0)
    z_slope = 0.5 * (zshift(1) - zshift(-1))
    y_slope = 0.5 * (yshift(1) - yshift(-1))
    z_fourth = zshift(2) - 4.0 * zshift(1) + 6.0 * centre - 4.0 * zshift(-1) + zshift(-2)
    y_fourth = yshift(2) - 4.0 * yshift(1) + 6.0 * centre - 4.0 * yshift(-1) + yshift(-2)
    damping = DISSIPATION * (z_fourth + y_fourth)
    density = centre[0] - COURANT * (MACH * z_slope[0] + z_slope[2] + y_slope[3]) - damping[0]
    pressure = centre[1] - COURANT * (MACH * z_slope[1] + z_slope[2] + y_slope[3]) - damping[1]
    along = centre[2] - COURANT * (MACH * z_slope[2] + z_slope[1]) - damping[2]
    normal = centre[3] - COURANT * (MACH * z_slope[3] + y_slope[1]) - damping[3]
    return jnp.stack([density, pressure, along, normal])


def with_rims(fields):
    return padded_2(fields, (("dom", 1),), 2)


def shards(disp_coarse, support_ids, rbf_weights, flow, pivots, lower_inverse, upper_inverse):
    block_size = disp_coarse.shape[0]
    domains = lax.axis_size("dom")
    coarse_table = lax.all_gather(
        disp_coarse.astype(jnp.bfloat16), "dom", axis=0, tiled=True
    ).reshape(domains, block_size)
    support = support_ids[0, 0]
    weights = rbf_weights[0, 0]
    matches = support[:, None] == lax.broadcasted_iota(jnp.int32, (support.shape[0], domains), 1)
    choose = matches.astype(jnp.bfloat16)
    picked = jnp.dot(choose, coarse_table, preferred_element_type=jnp.float32).astype(jnp.bfloat16)
    wall_motion = jnp.einsum("kj,kjz->z", picked, weights, preferred_element_type=jnp.float32)
    fields = flow[0].at[3, :, 0].set(wall_motion)
    for _ in range(ITERS):
        fields = stencil(with_rims(fields))
    push = (FACE_AREA * fields[1, :, 0]).astype(jnp.bfloat16)
    terms = jnp.einsum("kjz,z->kj", weights, push, preferred_element_type=jnp.float32)
    dense = jnp.einsum(
        "kb,kj->bj", matches.astype(jnp.float32), terms, precision=lax.Precision.HIGHEST
    )
    owned = lax.psum_scatter(dense, "dom", scatter_dimension=0, tiled=True)
    owned = lax.psum(owned, "sec")
    forces = lax.all_gather(owned, "dom", axis=0, tiled=True).reshape(-1)
    permuted = jnp.take(forces, pivots, axis=0)
    lower_part = jnp.dot(lower_inverse, permuted, precision=lax.Precision.HIGHEST)
    middle = lax.all_gather(lower_part, "dom", axis=0, tiled=True)
    solved = jnp.dot(upper_inverse, middle, precision=lax.Precision.HIGHEST)
    new_disp = 0.5 * disp_coarse + 0.5 * solved
    return (fields[None], new_disp)


def lane_index(shape):
    return lax.broadcasted_iota(jnp.int32, shape, 1)


def sweep(load, comps):
    shape = load(0, 0).shape
    lane = lane_index(shape)
    width = shape[1]

    def down(f, n):
        return jnp.where(lane >= n, pltpu.roll(f, n, 1), 0.0)

    def up(f, n):
        return jnp.where(lane < width - n, pltpu.roll(f, width - n, 1), 0.0)

    centre = [load(c, 0) for c in range(4)]
    need_y = set(comps) | ({3} if 0 in comps or 1 in comps else set()) | ({1} if 3 in comps else set())
    y_plus = {c: up(centre[c], 1) for c in need_y}
    y_minus = {c: down(centre[c], 1) for c in need_y}
    z_plus = [load(c, 1) for c in range(4)]
    z_minus = [load(c, -1) for c in range(4)]

    def z_slope(c):
        return 0.5 * (z_plus[c] - z_minus[c])

    def y_slope(c):
        return 0.5 * (y_plus[c] - y_minus[c])

    def damping(c):
        near = z_plus[c] + z_minus[c] + y_plus[c] + y_minus[c]
        far = load(c, 2) + load(c, -2) + up(centre[c], 2) + down(centre[c], 2)
        return DISSIPATION * (far - 4.0 * near + 12.0 * centre[c])

    out = {}
    if 0 in comps or 1 in comps:
        spread = z_slope(2) + y_slope(3)
    if 0 in comps:
        out[0] = centre[0] - COURANT * (MACH * z_slope(0) + spread) - damping(0)
    if 1 in comps:
        out[1] = centre[1] - COURANT * (MACH * z_slope(1) + spread) - damping(1)
    if 2 in comps:
        out[2] = centre[2] - COURANT * (MACH * z_slope(2) + z_slope(1)) - damping(2)
    if 3 in comps:
        out[3] = centre[3] - COURANT * (MACH * z_slope(3) + y_slope(1)) - damping(3)
    return out


def pack_body(
    halo, me_ref, ids_hbm, disp_hbm, flow_hbm, wt_hbm,
    near_ref, far_ref, own_ref, row_ref, ids_ref, flow_ref, wt_ref, sem,
):
    odd = me_ref[0] % 2 == 1
    comps, cells, width = flow_hbm.shape
    count = wt_hbm.shape[0]
    halves = wt_hbm.shape[2] // width
    deep = 2 * halo
    copies = [
        (flow_hbm.at[:, pl.ds(0, halo)], flow_ref.at[0]),
        (flow_hbm.at[:, pl.ds(cells - halo, halo)], flow_ref.at[1]),
        (wt_hbm.at[:, pl.ds(0, deep)], wt_ref.at[0]),
        (wt_hbm.at[:, pl.ds(cells - deep, deep)], wt_ref.at[1]),
        (ids_hbm, ids_ref),
        (disp_hbm, row_ref),
    ]
    copies = [pltpu.make_async_copy(src, dst, sem.at[i]) for i, (src, dst) in enumerate(copies)]
    for copy in copies:
        copy.start()
    for copy in copies:
        copy.wait()
    at = 0
    for c in range(comps):
        head, tail = flow_ref[0, c], flow_ref[1, c]
        near_ref[at : at + halo, :] = jnp.where(odd, head, tail)
        far_ref[at : at + halo, :] = jnp.where(odd, tail, head)
        at += halo
    for k in range(count):
        head = wt_ref[0, k].astype(jnp.float32)[0:halo]
        tail = wt_ref[1, k].astype(jnp.float32)[halo:deep]
        near = jnp.where(odd, head, tail)
        far = jnp.where(odd, tail, head)
        for h in range(halves):
            near_ref[at : at + halo, :] = near[:, h * width : (h + 1) * width]
            far_ref[at : at + halo, :] = far[:, h * width : (h + 1) * width]
            at += halo
    row = lax.broadcasted_iota(jnp.int32, (SUB, width), 0)
    ids = jnp.full((SUB, width), -1, jnp.int32)
    for k in range(count):
        ids = jnp.where(row == k, ids_ref[k], ids)
    ids = ids.astype(jnp.float32)
    near_ref[at : at + SUB, :] = ids
    far_ref[at : at + SUB, :] = ids
    own_ref[...] = ids[:, 0:LANES]


def still_body(halo, me_ref, near_ref, far_ref, flow_ref, still_ref, answer_ref, ping, pong):
    is_odd = me_ref[0] % 2 == 1
    _, cells, _ = flow_ref.shape

    def beside(load):
        group = lane_index((1, LANES)) // GROUP
        pressure, along, normal = [load(c)[:, 0:LANES] for c in (1, 2, 3)]
        packed = jnp.where(group == 1, pltpu.roll(along, GROUP, 1), pressure)
        return jnp.where(group == 2, pltpu.roll(normal, 2 * GROUP, 1), packed)

    at_near, at_far = [
        beside(lambda c: ref[c * halo : (c + 1) * halo, :]) for ref in (near_ref, far_ref)
    ]
    first = lane_index((1, LANES)) == 2 * GROUP
    parts = [
        (0, jnp.where(is_odd, at_near, at_far)),
        (halo, beside(lambda c: flow_ref[c])),
        (halo + cells, jnp.where(is_odd, at_far, at_near)),
    ]
    for at, part in parts:
        ping[SUB + at : SUB + at + part.shape[0], :] = jnp.where(first, 0.0, part)

    unit = SUB + cells + 3 * halo
    shape = (4 * halo, LANES)
    row = lax.broadcasted_iota(jnp.int32, shape, 0)
    ping[unit : unit + 4 * halo, :] = jnp.where((row == 2 * halo) & first, 1.0, 0.0)
    for ref in (ping, pong):
        ref[unit + 4 * halo :, :] = jnp.zeros((SUB, LANES), jnp.float32)
    ping[unit - halo : unit, :] = jnp.zeros((halo, LANES), jnp.float32)

    total = unit + 4 * halo - SUB
    src, dst = ping, pong
    for _ in range(ITERS):
        at, rows = SUB, total
        lane = lane_index((rows, LANES))
        group = lane // GROUP
        height = lane % GROUP
        centre = src[at : at + rows, :]
        z_plus, z_minus = [src[at + o : at + o + rows, :] for o in (1, -1)]
        y_plus = pltpu.roll(centre, LANES - 1, 1)
        y_minus = jnp.where(height >= 1, pltpu.roll(centre, 1, 1), 0.0)
        far_y = pltpu.roll(centre, LANES - 2, 1) + jnp.where(height >= 2, pltpu.roll(centre, 2, 1), 0.0)
        far_z = src[at + 2 : at + 2 + rows, :] + src[at - 2 : at - 2 + rows, :]
        damping = DISSIPATION * (
            far_y + far_z - 4.0 * (z_plus + z_minus + y_plus + y_minus) + 12.0 * centre
        )
        z_slope = 0.5 * (z_plus - z_minus)
        other_y = 0.5 * (
            pltpu.roll(centre, 2 * GROUP - 1, 1)
            - jnp.where(height >= 1, pltpu.roll(centre, 2 * GROUP + 1, 1), 0.0)
        )
        cross = jnp.where(group == 0, pltpu.roll(z_slope, LANES - GROUP, 1) + other_y, other_y)
        cross = jnp.where(group == 1, pltpu.roll(z_slope, GROUP, 1), cross)
        value = centre - COURANT * (MACH * z_slope + cross) - damping
        dst[at : at + rows, :] = jnp.where(group == 3, 0.0, value)
        src, dst = dst, src
    still_ref[...] = jnp.broadcast_to(src[SUB + halo : SUB + halo + cells, 0:1], still_ref.shape)
    answer_ref[...] = jnp.broadcast_to(
        src[unit + halo : unit + halo + answer_ref.shape[0], 0:1], answer_ref.shape
    )


def wall_body(
    halo, me_ref, ids_ref, mine_ref, theirs_ref, own_ref, near_ref, far_ref, still_ref, answer_ref,
    wt_ref, pivots_ref, wall_ref, permuted_ref,
):
    me = me_ref[0]
    odd = me % 2
    is_odd = odd == 1
    chips = mine_ref.shape[0]
    cells, width = still_ref.shape[0], near_ref.shape[1]
    count, _, block = wt_ref.shape
    halves = block // width
    comps = (near_ref.shape[0] - SUB) // halo - count * halves
    ids_at = halo * (comps + count * halves)

    slot = lax.broadcasted_iota(jnp.int32, (SUB * 3, 2 * chips), 1)
    chip = (me // 2) ^ (slot % chips)
    core = odd ^ (slot // chips)
    block_of = (2 * chip + core).astype(jnp.float32)
    ids = jnp.concatenate(
        [own_ref[:, 0:1], near_ref[ids_at : ids_at + SUB, 0:1], far_ref[ids_at : ids_at + SUB, 0:1]],
        axis=0,
    )
    choose = (ids == block_of).astype(jnp.bfloat16)
    table = jnp.concatenate([mine_ref[...], theirs_ref[...]], axis=0).astype(jnp.bfloat16)
    picked = jnp.dot(choose, table, preferred_element_type=jnp.float32)

    own = jnp.zeros((cells, LANES), jnp.float32)
    edge = [jnp.zeros((halo, LANES), jnp.float32) for _ in range(2)]
    for k in range(count):
        weights = wt_ref[k].astype(jnp.float32)
        for q in range(0, block, LANES):
            own += weights[:, q : q + LANES] * picked[k : k + 1, q : q + LANES]
            rows = halo * (comps + k * halves + q // width)
            for e, ref in enumerate((near_ref, far_ref)):
                edge[e] += (
                    ref[rows : rows + halo, q % width : q % width + LANES]
                    * picked[SUB * (e + 1) + k : SUB * (e + 1) + k + 1, q : q + LANES]
                )
    own = jnp.sum(own, axis=1, keepdims=True)
    near, far = [jnp.sum(e, axis=1, keepdims=True) for e in edge]

    for at, column in (
        (0, jnp.where(is_odd, near, far)),
        (halo, own),
        (halo + cells, jnp.where(is_odd, far, near)),
    ):
        rows = column.shape[0]
        wall_ref[at : at + rows, :] = jnp.broadcast_to(column, (rows, LANES))
    value = still_ref[...]
    for m in range(2 * halo + 1):
        value = value + answer_ref[m : m + 1, :] * wall_ref[2 * halo - m : 2 * halo - m + cells, :]
    push = (FACE_AREA * value).astype(jnp.bfloat16).astype(jnp.float32)

    pivot = pivots_ref[...]
    row = jnp.right_shift(pivot, LANES.bit_length() - 1)
    lane = jnp.bitwise_and(pivot, LANES - 1)
    got = jnp.zeros(pivot.shape, jnp.float32)
    for k in range(count):
        weights = wt_ref[k].astype(jnp.float32)
        for q in range(block // LANES):
            term = jnp.sum(weights[:, q * LANES : (q + 1) * LANES] * push, axis=0, keepdims=True)
            source = jnp.take_along_axis(jnp.broadcast_to(term, pivot.shape), lane, axis=1)
            got = jnp.where(row == ids_ref[k] * (block // LANES) + q, source, got)
    permuted_ref[...] = got


def flow_body(
    halo, me_ref, near_ref, far_ref, flow_hbm, wall_ref, front_hbm, out_ref, tail_ref, ping, pong, sem
):
    left = front_hbm.shape[1] - tail_ref.shape[1]
    fetch = pltpu.make_async_copy(front_hbm.at[:, pl.ds(left, tail_ref.shape[1])], tail_ref, sem.at[0])
    fetch.start()
    is_odd = me_ref[0] % 2 == 1
    comps, cells, width = flow_hbm.shape
    middle = SUB + halo
    field = pltpu.make_async_copy(flow_hbm, ping.at[:, pl.ds(middle, cells)], sem.at[1])
    field.start()
    lane = lane_index((1, width))
    for c in range(comps):
        near = near_ref[c * halo : (c + 1) * halo, :]
        far = far_ref[c * halo : (c + 1) * halo, :]
        for at, part in ((0, jnp.where(is_odd, near, far)), (halo + cells, jnp.where(is_odd, far, near))):
            if c == comps - 1:
                part = jnp.where(lane == 0, wall_ref[at : at + halo, 0:1], part)
            ping[c, SUB + at : SUB + at + halo, :] = part
    field.wait()
    wall = wall_ref[halo : halo + cells, :]
    normal = ping[comps - 1, middle : middle + cells, 0:LANES]
    ping[comps - 1, middle : middle + cells, 0:LANES] = jnp.where(lane_index((1, LANES)) == 0, wall, normal)
    src, dst = ping, pong
    extent = cells + 2 * halo
    for index in range(ITERS):
        last = index == ITERS - 1
        first = halo if last else 0
        total = cells if last else extent
        step = 16
        for at in range(first, first + total, step):
            base = SUB + at
            out = sweep(lambda c, o: src[c, base + o : base + o + step, :], (0, 1, 2, 3))
            for c, value in out.items():
                if last:
                    out_ref[c, at - halo : at - halo + step, :] = value
                else:
                    dst[c, base : base + step, :] = value
        src, dst = dst, src
    fetch.wait()


def spread_rows(columns, row_of):
    return [jnp.broadcast_to(row_of(c), (SUB, LANES)) for c in range(columns // LANES)]


def front_product(front_ref, spread):
    rows, columns = front_ref.shape
    out = []
    for top in range(0, rows, LANES):
        parts = []
        for at in range(top, top + LANES, SUB):
            total = None
            for c in range(columns // LANES):
                term = front_ref[at : at + SUB, c * LANES : (c + 1) * LANES] * spread[c]
                total = term if total is None else total + term
            parts.append(total)
        out.append(jnp.sum(jnp.concatenate(parts, axis=0).T, axis=0, keepdims=True))
    return jnp.concatenate(out, axis=1)


def lower_body(parts, *refs):
    front_ref, out_ref, permuted = refs[parts:]
    total = refs[0][...]
    for ref in refs[1:parts]:
        total = total + ref[...]
    permuted[...] = total
    spread = spread_rows(front_ref.shape[1], lambda c: permuted[c : c + 1, :])
    result = front_product(front_ref, spread)
    out_ref[...] = jnp.broadcast_to(result[None], out_ref.shape)


def upper_body(
    sections, me_ref, parts_ref, disp_hbm, tail_ref, front_hbm, out_ref, disp_ref, head_ref, total, sem
):
    me = me_ref[0]
    block = parts_ref.shape[2]
    domains = parts_ref.shape[0] // sections
    heads = head_ref.shape[0]
    copies = [
        pltpu.make_async_copy(
            front_hbm.at[:, pl.ds(b * block, block)], head_ref.at[b], sem.at[b]
        )
        for b in range(heads)
    ]
    own = pltpu.make_async_copy(disp_hbm, disp_ref, sem.at[heads])
    own.start()
    for b in reversed(range(heads)):
        pl.when(b >= me)(copies[b].start)
    total[...] = jnp.zeros_like(total)
    for b in reversed(range(domains)):

        def add(b=b):
            if b < heads:
                copies[b].wait()
            rows = []
            for q in range(0, block, LANES):
                first = (domains - 1 - b) * sections
                part = parts_ref[first, :, q : q + LANES]
                for s in range(1, sections):
                    part = part + parts_ref[first + s, :, q : q + LANES]
                rows.append(jnp.broadcast_to(part, (SUB, LANES)))
            for at in range(0, block, SUB):
                value = total[at : at + SUB, :]
                for i, row in enumerate(rows):
                    if b < heads:
                        front = head_ref[b, at : at + SUB, i * LANES : (i + 1) * LANES]
                    else:
                        left = (b - heads) * block + i * LANES
                        front = tail_ref[at : at + SUB, left : left + LANES]
                    value = value + front * row
                total[at : at + SUB, :] = value

        pl.when(b >= me)(add)
    solved = [
        jnp.sum(total[at : at + LANES, :].T, axis=0, keepdims=True) for at in range(0, block, LANES)
    ]
    own.wait()
    out_ref[...] = 0.5 * disp_ref[...] + 0.5 * jnp.concatenate(solved, axis=1)


VMEM = pl.BlockSpec(memory_space=pltpu.VMEM)
SMEM = pl.BlockSpec(memory_space=pltpu.SMEM)
HBM = pl.BlockSpec(memory_space=pltpu.HBM)

COVER = 20_000_000_000

TAIL_BYTES = 2 << 20


def call(body, in_specs, out_shape, scratch, cost, limit):
    many = isinstance(out_shape, tuple)
    return pl.pallas_call(
        body,
        out_shape=out_shape,
        in_specs=in_specs,
        out_specs=(VMEM,) * len(out_shape) if many else VMEM,
        scratch_shapes=scratch,
        compiler_params=pltpu.CompilerParams(vmem_limit_bytes=limit),
        cost_estimate=pl.CostEstimate(flops=cost[0], bytes_accessed=cost[1], transcendentals=0),
    )


def in_hbm(array):
    return pltpu.with_memory_space_constraint(array, pltpu.HBM)


def f32(*shape):
    return jax.ShapeDtypeStruct(shape, jnp.float32)


def fast_shards(disp_coarse, support_ids, rbf_weights, flow, pivots, lower_inverse, upper_inverse):
    block = disp_coarse.shape[0]
    sections, domains = lax.axis_size("sec"), lax.axis_size("dom")
    chips = domains // 2
    halo = REACH * ITERS
    me = lax.axis_index("dom").astype(jnp.int32).reshape(1)
    ids = support_ids[0, 0]
    weights = jnp.swapaxes(rbf_weights[0, 0], 1, 2)
    field = flow[0]
    count, cells, _ = weights.shape
    comps, _, width = field.shape

    def across(array, k):
        return lax.ppermute(array, "dom", [(i, i ^ (2 * k)) for i in range(domains)])

    def partner(array):
        return lax.ppermute(array, "dom", [(i, i ^ 1) for i in range(domains)])

    def neighbour(array):
        pairs = [(i, (i + 1) % domains if i % 2 else (i - 1) % domains) for i in range(domains)]
        return lax.ppermute(array, "dom", pairs)

    row = disp_coarse.reshape(1, block)
    rows = halo * comps + halo * count * (block // width) + SUB
    near, far, own, mine = call(
        functools.partial(pack_body, halo),
        [SMEM] + [HBM] * 4,
        (f32(rows, width), f32(rows, width), f32(SUB, LANES), f32(1, block)),
        [
            pltpu.SMEM((count,), jnp.int32),
            pltpu.VMEM((2, comps, halo, width), jnp.float32),
            pltpu.VMEM((2, count, 2 * halo, block), weights.dtype),
            pltpu.SemaphoreType.DMA((6,)),
        ],
        (COVER, 400_000),
        4 << 20,
    )(me, *[in_hbm(x) for x in (ids, row, field, weights)])
    far = neighbour(far)
    near = partner(near)
    others = []
    for k in range(1, chips):
        others.append(across(row if k == chips - 1 else mine, k))
    mine = jnp.concatenate([mine] + others, axis=0)
    theirs = partner(mine)

    extent = cells + 2 * halo
    still, answer = call(
        functools.partial(still_body, halo),
        [SMEM] + [VMEM] * 3,
        (f32(cells, LANES), f32(3 * halo, LANES)),
        [pltpu.VMEM((cells + 7 * halo + 2 * SUB, LANES), jnp.float32)] * 2,
        (COVER, 40_000_000),
        4 << 20,
    )(me, near, far, field)
    pivot_rows = pivots.reshape(-1, LANES)
    wall, permuted = call(
        functools.partial(wall_body, halo),
        [SMEM, SMEM] + [VMEM] * 9,
        (f32(extent, LANES), f32(*pivot_rows.shape)),
        [],
        (COVER, 40_000_000),
        4 << 20,
    )(me, ids, mine, theirs, own, near, far, still, answer, weights, pivot_rows)

    pair = permuted + partner(permuted)
    pieces = [pair] + [across(pair, k) for k in range(chips - 1, 0, -1)]
    tails = max(1, min(domains - 1, TAIL_BYTES // (4 * block * block)))
    new_flow, tail = call(
        functools.partial(flow_body, halo),
        [SMEM, VMEM, VMEM, HBM, VMEM, HBM],
        (f32(comps, cells, width), f32(block, tails * block)),
        [pltpu.VMEM((comps, extent + 2 * SUB, width), jnp.float32)] * 2
        + [pltpu.SemaphoreType.DMA((2,))],
        (COVER, 4_000_000),
        8 << 20,
    )(me, near, far, in_hbm(field), wall, in_hbm(upper_inverse))

    lower = call(
        functools.partial(lower_body, len(pieces)),
        [VMEM] * (len(pieces) + 1),
        f32(sections * domains, 1, block),
        [pltpu.VMEM(pivot_rows.shape, jnp.float32)],
        (COVER, 1_000_000),
        4 << 20,
    )(*pieces, lower_inverse)
    order = [s * domains + d for d in reversed(range(domains)) for s in range(sections)]
    middle = lax.all_to_all(
        lower, ("sec", "dom"), 0, 0, axis_index_groups=[order], tiled=True
    )
    new_disp = call(
        functools.partial(upper_body, sections),
        [SMEM, VMEM, HBM, VMEM, HBM],
        f32(1, block),
        [
            pltpu.VMEM((1, block), jnp.float32),
            pltpu.VMEM((domains - tails, block, block), jnp.float32),
            pltpu.VMEM((block, LANES), jnp.float32),
            pltpu.SemaphoreType.DMA((domains - tails + 1,)),
        ],
        (COVER, 1_000_000),
        12 << 20,
    )(me, middle, in_hbm(row), tail, in_hbm(upper_inverse))
    return (new_flow[None], new_disp.reshape(block))


def fits(mesh):
    chips, odd = divmod(mesh.shape["dom"], 2)
    return odd == 0 and chips & (chips - 1) == 0 and 1 < chips <= 8


def body_for(mesh):
    def body(disp_coarse, support_ids, rbf_weights, flow, pivots, lower_inverse, upper_inverse):
        args = (disp_coarse, support_ids, rbf_weights, flow, pivots, lower_inverse, upper_inverse)
        block = disp_coarse.shape[0]
        cells, width = flow.shape[2:]
        halo = REACH * ITERS
        small = (
            block % width == 0
            and width % LANES == 0
            and cells % (4 * halo) == 0
            and halo == SUB
            and 2 * halo < GROUP
            and flow.shape[1] == 4
            and pivots.shape[0] % (SUB * LANES) == 0
            and support_ids.shape[2] <= SUB
        )
        return fast_shards(*args) if fits(mesh) and small else shards(*args)

    return body


def solution(mesh):
    return jax.shard_map(
        body_for(mesh),
        mesh=mesh,
        in_specs=(
            P("dom"),
            P("sec", "dom", None),
            P("sec", "dom", None, None, None),
            P("sec", None, "dom", None),
            P(),
            P("dom", None),
            P("dom", None),
        ),
        out_specs=(P("sec", None, "dom", None), P("dom")),
        check_vma=False,
    )
```

```python
import functools

import jax
import jax.numpy as jnp
from jax import lax
from jax.experimental import pallas as pl
from jax.experimental.pallas import tpu as pltpu
from jax.sharding import PartitionSpec as P


ITERS = 4
REACH = 2


COURANT = 0.4
MACH = 0.5
DISSIPATION = 0.03125
FACE_AREA = 0.125

LANES = 128
SUB = 8
GROUP = LANES // 4


def padded_2(cells, sides, width):
    for axis, dim in sides:
        count = lax.axis_size(axis)
        head = lax.slice_in_dim(cells, 0, width, axis=dim)
        tail = lax.slice_in_dim(cells, cells.shape[dim] - width, cells.shape[dim], axis=dim)
        cells = jnp.concatenate(
            [
                lax.ppermute(tail, axis, [(i, (i + 1) % count) for i in range(count)]),
                cells,
                lax.ppermute(head, axis, [((i + 1) % count, i) for i in range(count)]),
            ],
            axis=dim,
        )
    return cells


def stencil(padded):
    z_extent = padded.shape[1]
    y_extent = padded.shape[2]
    y_padded = jnp.pad(padded, ((0, 0), (0, 0), (2, 2)))

    def zshift(offset):
        return y_padded[:, 2 + offset : z_extent - 2 + offset, 2 : y_extent + 2]

    def yshift(offset):
        return y_padded[:, 2 : z_extent - 2, 2 + offset : y_extent + 2 + offset]

    centre = zshift(0)
    z_slope = 0.5 * (zshift(1) - zshift(-1))
    y_slope = 0.5 * (yshift(1) - yshift(-1))
    z_fourth = zshift(2) - 4.0 * zshift(1) + 6.0 * centre - 4.0 * zshift(-1) + zshift(-2)
    y_fourth = yshift(2) - 4.0 * yshift(1) + 6.0 * centre - 4.0 * yshift(-1) + yshift(-2)
    damping = DISSIPATION * (z_fourth + y_fourth)
    density = centre[0] - COURANT * (MACH * z_slope[0] + z_slope[2] + y_slope[3]) - damping[0]
    pressure = centre[1] - COURANT * (MACH * z_slope[1] + z_slope[2] + y_slope[3]) - damping[1]
    along = centre[2] - COURANT * (MACH * z_slope[2] + z_slope[1]) - damping[2]
    normal = centre[3] - COURANT * (MACH * z_slope[3] + y_slope[1]) - damping[3]
    return jnp.stack([density, pressure, along, normal])


def with_rims(fields):
    return padded_2(fields, (("dom", 1),), 2)


def shards(disp_coarse, support_ids, rbf_weights, flow, pivots, lower_inverse, upper_inverse):
    block_size = disp_coarse.shape[0]
    domains = lax.axis_size("dom")
    coarse_table = lax.all_gather(
        disp_coarse.astype(jnp.bfloat16), "dom", axis=0, tiled=True
    ).reshape(domains, block_size)
    support = support_ids[0, 0]
    weights = rbf_weights[0, 0]
    matches = support[:, None] == lax.broadcasted_iota(jnp.int32, (support.shape[0], domains), 1)
    choose = matches.astype(jnp.bfloat16)
    picked = jnp.dot(choose, coarse_table, preferred_element_type=jnp.float32).astype(jnp.bfloat16)
    wall_motion = jnp.einsum("kj,kjz->z", picked, weights, preferred_element_type=jnp.float32)
    fields = flow[0].at[3, :, 0].set(wall_motion)
    for _ in range(ITERS):
        fields = stencil(with_rims(fields))
    push = (FACE_AREA * fields[1, :, 0]).astype(jnp.bfloat16)
    terms = jnp.einsum("kjz,z->kj", weights, push, preferred_element_type=jnp.float32)
    dense = jnp.einsum(
        "kb,kj->bj", matches.astype(jnp.float32), terms, precision=lax.Precision.HIGHEST
    )
    owned = lax.psum_scatter(dense, "dom", scatter_dimension=0, tiled=True)
    owned = lax.psum(owned, "sec")
    forces = lax.all_gather(owned, "dom", axis=0, tiled=True).reshape(-1)
    permuted = jnp.take(forces, pivots, axis=0)
    lower_part = jnp.dot(lower_inverse, permuted, precision=lax.Precision.HIGHEST)
    middle = lax.all_gather(lower_part, "dom", axis=0, tiled=True)
    solved = jnp.dot(upper_inverse, middle, precision=lax.Precision.HIGHEST)
    new_disp = 0.5 * disp_coarse + 0.5 * solved
    return (fields[None], new_disp)


def lane_index(shape):
    return lax.broadcasted_iota(jnp.int32, shape, 1)


def sweep(load, comps):
    shape = load(0, 0).shape
    lane = lane_index(shape)
    width = shape[1]

    def down(f, n):
        return jnp.where(lane >= n, pltpu.roll(f, n, 1), 0.0)

    def up(f, n):
        return jnp.where(lane < width - n, pltpu.roll(f, width - n, 1), 0.0)

    centre = [load(c, 0) for c in range(4)]
    need_y = set(comps) | ({3} if 0 in comps or 1 in comps else set()) | ({1} if 3 in comps else set())
    y_plus = {c: up(centre[c], 1) for c in need_y}
    y_minus = {c: down(centre[c], 1) for c in need_y}
    z_plus = [load(c, 1) for c in range(4)]
    z_minus = [load(c, -1) for c in range(4)]

    def z_slope(c):
        return 0.5 * (z_plus[c] - z_minus[c])

    def y_slope(c):
        return 0.5 * (y_plus[c] - y_minus[c])

    def damping(c):
        near = z_plus[c] + z_minus[c] + y_plus[c] + y_minus[c]
        far = load(c, 2) + load(c, -2) + up(centre[c], 2) + down(centre[c], 2)
        return DISSIPATION * (far - 4.0 * near + 12.0 * centre[c])

    out = {}
    if 0 in comps or 1 in comps:
        spread = z_slope(2) + y_slope(3)
    if 0 in comps:
        out[0] = centre[0] - COURANT * (MACH * z_slope(0) + spread) - damping(0)
    if 1 in comps:
        out[1] = centre[1] - COURANT * (MACH * z_slope(1) + spread) - damping(1)
    if 2 in comps:
        out[2] = centre[2] - COURANT * (MACH * z_slope(2) + z_slope(1)) - damping(2)
    if 3 in comps:
        out[3] = centre[3] - COURANT * (MACH * z_slope(3) + y_slope(1)) - damping(3)
    return out


def pack_body(
    halo, me_ref, ids_hbm, disp_hbm, flow_hbm, wt_hbm,
    near_ref, far_ref, own_ref, row_ref, ids_ref, flow_ref, wt_ref, sem,
):
    odd = me_ref[0] % 2 == 1
    comps, cells, width = flow_hbm.shape
    count = wt_hbm.shape[0]
    halves = wt_hbm.shape[2] // width
    deep = 2 * halo
    copies = [
        (flow_hbm.at[:, pl.ds(0, halo)], flow_ref.at[0]),
        (flow_hbm.at[:, pl.ds(cells - halo, halo)], flow_ref.at[1]),
        (wt_hbm.at[:, pl.ds(0, deep)], wt_ref.at[0]),
        (wt_hbm.at[:, pl.ds(cells - deep, deep)], wt_ref.at[1]),
        (ids_hbm, ids_ref),
        (disp_hbm, row_ref),
    ]
    copies = [pltpu.make_async_copy(src, dst, sem.at[i]) for i, (src, dst) in enumerate(copies)]
    for copy in copies:
        copy.start()
    for copy in copies:
        copy.wait()
    at = 0
    for c in range(comps):
        head, tail = flow_ref[0, c], flow_ref[1, c]
        near_ref[at : at + halo, :] = jnp.where(odd, head, tail)
        far_ref[at : at + halo, :] = jnp.where(odd, tail, head)
        at += halo
    for k in range(count):
        head = wt_ref[0, k].astype(jnp.float32)[0:halo]
        tail = wt_ref[1, k].astype(jnp.float32)[halo:deep]
        near = jnp.where(odd, head, tail)
        far = jnp.where(odd, tail, head)
        for h in range(halves):
            near_ref[at : at + halo, :] = near[:, h * width : (h + 1) * width]
            far_ref[at : at + halo, :] = far[:, h * width : (h + 1) * width]
            at += halo
    row = lax.broadcasted_iota(jnp.int32, (SUB, width), 0)
    ids = jnp.full((SUB, width), -1, jnp.int32)
    for k in range(count):
        ids = jnp.where(row == k, ids_ref[k], ids)
    ids = ids.astype(jnp.float32)
    near_ref[at : at + SUB, :] = ids
    far_ref[at : at + SUB, :] = ids
    own_ref[...] = ids[:, 0:LANES]


def still_body(halo, me_ref, near_ref, far_ref, flow_ref, still_ref, answer_ref, ping, pong):
    is_odd = me_ref[0] % 2 == 1
    _, cells, _ = flow_ref.shape

    def beside(load):
        group = lane_index((1, LANES)) // GROUP
        pressure, along, normal = [load(c)[:, 0:LANES] for c in (1, 2, 3)]
        packed = jnp.where(group == 1, pltpu.roll(along, GROUP, 1), pressure)
        return jnp.where(group == 2, pltpu.roll(normal, 2 * GROUP, 1), packed)

    at_near, at_far = [
        beside(lambda c: ref[c * halo : (c + 1) * halo, :]) for ref in (near_ref, far_ref)
    ]
    first = lane_index((1, LANES)) == 2 * GROUP
    parts = [
        (0, jnp.where(is_odd, at_near, at_far)),
        (halo, beside(lambda c: flow_ref[c])),
        (halo + cells, jnp.where(is_odd, at_far, at_near)),
    ]
    for at, part in parts:
        ping[SUB + at : SUB + at + part.shape[0], :] = jnp.where(first, 0.0, part)

    unit = SUB + cells + 3 * halo
    shape = (4 * halo, LANES)
    row = lax.broadcasted_iota(jnp.int32, shape, 0)
    ping[unit : unit + 4 * halo, :] = jnp.where((row == 2 * halo) & first, 1.0, 0.0)
    for ref in (ping, pong):
        ref[unit + 4 * halo :, :] = jnp.zeros((SUB, LANES), jnp.float32)
    ping[unit - halo : unit, :] = jnp.zeros((halo, LANES), jnp.float32)

    total = unit + 4 * halo - SUB
    src, dst = ping, pong
    for _ in range(ITERS):
        at, rows = SUB, total
        lane = lane_index((rows, LANES))
        group = lane // GROUP
        height = lane % GROUP
        centre = src[at : at + rows, :]
        z_plus, z_minus = [src[at + o : at + o + rows, :] for o in (1, -1)]
        y_plus = pltpu.roll(centre, LANES - 1, 1)
        y_minus = jnp.where(height >= 1, pltpu.roll(centre, 1, 1), 0.0)
        far_y = pltpu.roll(centre, LANES - 2, 1) + jnp.where(height >= 2, pltpu.roll(centre, 2, 1), 0.0)
        far_z = src[at + 2 : at + 2 + rows, :] + src[at - 2 : at - 2 + rows, :]
        damping = DISSIPATION * (
            far_y + far_z - 4.0 * (z_plus + z_minus + y_plus + y_minus) + 12.0 * centre
        )
        z_slope = 0.5 * (z_plus - z_minus)
        other_y = 0.5 * (
            pltpu.roll(centre, 2 * GROUP - 1, 1)
            - jnp.where(height >= 1, pltpu.roll(centre, 2 * GROUP + 1, 1), 0.0)
        )
        cross = jnp.where(group == 0, pltpu.roll(z_slope, LANES - GROUP, 1) + other_y, other_y)
        cross = jnp.where(group == 1, pltpu.roll(z_slope, GROUP, 1), cross)
        value = centre - COURANT * (MACH * z_slope + cross) - damping
        dst[at : at + rows, :] = jnp.where(group == 3, 0.0, value)
        src, dst = dst, src
    still_ref[...] = jnp.broadcast_to(src[SUB + halo : SUB + halo + cells, 0:1], still_ref.shape)
    answer_ref[...] = jnp.broadcast_to(
        src[unit + halo : unit + halo + answer_ref.shape[0], 0:1], answer_ref.shape
    )


def wall_body(
    halo, me_ref, ids_ref, mine_ref, theirs_ref, own_ref, near_ref, far_ref, still_ref, answer_ref,
    wt_ref, pivots_ref, wall_ref, permuted_ref,
):
    me = me_ref[0]
    odd = me % 2
    is_odd = odd == 1
    chips = mine_ref.shape[0]
    cells, width = still_ref.shape[0], near_ref.shape[1]
    count, _, block = wt_ref.shape
    halves = block // width
    comps = (near_ref.shape[0] - SUB) // halo - count * halves
    ids_at = halo * (comps + count * halves)

    slot = lax.broadcasted_iota(jnp.int32, (SUB * 3, 2 * chips), 1)
    chip = (me // 2) ^ (slot % chips)
    core = odd ^ (slot // chips)
    block_of = (2 * chip + core).astype(jnp.float32)
    ids = jnp.concatenate(
        [own_ref[:, 0:1], near_ref[ids_at : ids_at + SUB, 0:1], far_ref[ids_at : ids_at + SUB, 0:1]],
        axis=0,
    )
    choose = (ids == block_of).astype(jnp.bfloat16)
    table = jnp.concatenate([mine_ref[...], theirs_ref[...]], axis=0).astype(jnp.bfloat16)
    picked = jnp.dot(choose, table, preferred_element_type=jnp.float32)

    own = jnp.zeros((cells, LANES), jnp.float32)
    edge = [jnp.zeros((halo, LANES), jnp.float32) for _ in range(2)]
    for k in range(count):
        weights = wt_ref[k].astype(jnp.float32)
        for q in range(0, block, LANES):
            own += weights[:, q : q + LANES] * picked[k : k + 1, q : q + LANES]
            rows = halo * (comps + k * halves + q // width)
            for e, ref in enumerate((near_ref, far_ref)):
                edge[e] += (
                    ref[rows : rows + halo, q % width : q % width + LANES]
                    * picked[SUB * (e + 1) + k : SUB * (e + 1) + k + 1, q : q + LANES]
                )
    own = jnp.sum(own, axis=1, keepdims=True)
    near, far = [jnp.sum(e, axis=1, keepdims=True) for e in edge]

    for at, column in (
        (0, jnp.where(is_odd, near, far)),
        (halo, own),
        (halo + cells, jnp.where(is_odd, far, near)),
    ):
        rows = column.shape[0]
        wall_ref[at : at + rows, :] = jnp.broadcast_to(column, (rows, LANES))
    value = still_ref[...]
    for m in range(2 * halo + 1):
        value = value + answer_ref[m : m + 1, :] * wall_ref[2 * halo - m : 2 * halo - m + cells, :]
    push = (FACE_AREA * value).astype(jnp.bfloat16).astype(jnp.float32)

    pivot = pivots_ref[...]
    row = jnp.right_shift(pivot, LANES.bit_length() - 1)
    lane = jnp.bitwise_and(pivot, LANES - 1)
    got = jnp.zeros(pivot.shape, jnp.float32)
    for k in range(count):
        weights = wt_ref[k].astype(jnp.float32)
        for q in range(block // LANES):
            term = jnp.sum(weights[:, q * LANES : (q + 1) * LANES] * push, axis=0, keepdims=True)
            source = jnp.take_along_axis(jnp.broadcast_to(term, pivot.shape), lane, axis=1)
            got = jnp.where(row == ids_ref[k] * (block // LANES) + q, source, got)
    permuted_ref[...] = got


def full_sweep(src, dst, first, rows, shift):
    step = 16
    for at in range(first, first + rows, step):
        out = sweep(lambda c, o: src[c, at + o : at + o + step, :], (0, 1, 2, 3))
        for c, value in out.items():
            dst[c, at - shift : at - shift + step, :] = value


def early_body(halo, me_ref, near_ref, far_ref, flow_ref, wall_ref, out_ref, ping, pong):
    is_odd = me_ref[0] % 2 == 1
    comps, cells, width = flow_ref.shape
    lane = lane_index((1, width))
    for c in range(comps):
        near = near_ref[c * halo : (c + 1) * halo, :]
        far = far_ref[c * halo : (c + 1) * halo, :]
        parts = [
            (0, jnp.where(is_odd, near, far)),
            (halo, flow_ref[c]),
            (halo + cells, jnp.where(is_odd, far, near)),
        ]
        for at, part in parts:
            rows = part.shape[0]
            if c == comps - 1:
                part = jnp.where(lane == 0, wall_ref[at : at + rows, 0:1], part)
            ping[c, SUB + at : SUB + at + rows, :] = part
    extent = cells + 2 * halo
    refs = (ping, pong)
    for index in range(ITERS // 2):
        dst = out_ref if index == ITERS // 2 - 1 else refs[(index + 1) % 2]
        full_sweep(refs[index % 2], dst, SUB, extent, 0)


def late_body(halo, field_ref, out_ref, ping, pong):
    _, cells, _ = out_ref.shape
    extent = cells + 2 * halo
    src, refs = field_ref, (ping, pong)
    for index in range(ITERS // 2, ITERS):
        if index == ITERS - 1:
            full_sweep(src, out_ref, SUB + halo, cells, SUB + halo)
        else:
            full_sweep(src, refs[index % 2], SUB, extent, 0)
            src = refs[index % 2]


def spread_rows(columns, row_of):
    return [jnp.broadcast_to(row_of(c), (SUB, LANES)) for c in range(columns // LANES)]


def front_product(front_ref, spread):
    rows, columns = front_ref.shape
    out = []
    for top in range(0, rows, LANES):
        parts = []
        for at in range(top, top + LANES, SUB):
            total = None
            for c in range(columns // LANES):
                term = front_ref[at : at + SUB, c * LANES : (c + 1) * LANES] * spread[c]
                total = term if total is None else total + term
            parts.append(total)
        out.append(jnp.sum(jnp.concatenate(parts, axis=0).T, axis=0, keepdims=True))
    return jnp.concatenate(out, axis=1)


def lower_body(parts, *refs):
    front_ref, out_ref, permuted = refs[parts:]
    total = refs[0][...]
    for ref in refs[1:parts]:
        total = total + ref[...]
    permuted[...] = total
    spread = spread_rows(front_ref.shape[1], lambda c: permuted[c : c + 1, :])
    result = front_product(front_ref, spread)
    out_ref[...] = result


def upper_body(parts, me_ref, *refs):
    disp_ref, front_ref, out_ref, table = refs[parts:]
    me = me_ref[0]
    block = table.shape[1]
    for k in range(parts):
        table[2 * k : 2 * k + 2, :] = refs[k][...]
    rows = []
    for b in range(2 * parts):
        at = 2 * ((b // 2) ^ (me // 2)) + ((b % 2) ^ (me % 2))
        row = table[pl.ds(at, 1), :]
        rows += [row[:, q : q + LANES] for q in range(0, block, LANES)]
    solved = front_product(front_ref, spread_rows(front_ref.shape[1], lambda c: rows[c]))
    out_ref[...] = 0.5 * disp_ref[...] + 0.5 * solved


VMEM = pl.BlockSpec(memory_space=pltpu.VMEM)
SMEM = pl.BlockSpec(memory_space=pltpu.SMEM)
HBM = pl.BlockSpec(memory_space=pltpu.HBM)

COVER = 20_000_000_000


def call(body, in_specs, out_shape, scratch, cost, limit):
    many = isinstance(out_shape, tuple)
    return pl.pallas_call(
        body,
        out_shape=out_shape,
        in_specs=in_specs,
        out_specs=(VMEM,) * len(out_shape) if many else VMEM,
        scratch_shapes=scratch,
        compiler_params=pltpu.CompilerParams(vmem_limit_bytes=limit),
        cost_estimate=pl.CostEstimate(flops=cost[0], bytes_accessed=cost[1], transcendentals=0),
    )


def in_hbm(array):
    return pltpu.with_memory_space_constraint(array, pltpu.HBM)


def f32(*shape):
    return jax.ShapeDtypeStruct(shape, jnp.float32)


def fast_shards(disp_coarse, support_ids, rbf_weights, flow, pivots, lower_inverse, upper_inverse):
    block = disp_coarse.shape[0]
    sections, domains = lax.axis_size("sec"), lax.axis_size("dom")
    chips = domains // 2
    halo = REACH * ITERS
    me = lax.axis_index("dom").astype(jnp.int32).reshape(1)
    ids = support_ids[0, 0]
    weights = jnp.swapaxes(rbf_weights[0, 0], 1, 2)
    field = flow[0]
    count, cells, _ = weights.shape
    comps, _, width = field.shape

    def across(array, k):
        return lax.ppermute(array, "dom", [(i, i ^ (2 * k)) for i in range(domains)])

    def partner(array):
        return lax.ppermute(array, "dom", [(i, i ^ 1) for i in range(domains)])

    def neighbour(array):
        pairs = [(i, (i + 1) % domains if i % 2 else (i - 1) % domains) for i in range(domains)]
        return lax.ppermute(array, "dom", pairs)

    row = disp_coarse.reshape(1, block)
    rows = halo * comps + halo * count * (block // width) + SUB
    near, far, own, mine = call(
        functools.partial(pack_body, halo),
        [SMEM] + [HBM] * 4,
        (f32(rows, width), f32(rows, width), f32(SUB, LANES), f32(1, block)),
        [
            pltpu.SMEM((count,), jnp.int32),
            pltpu.VMEM((2, comps, halo, width), jnp.float32),
            pltpu.VMEM((2, count, 2 * halo, block), weights.dtype),
            pltpu.SemaphoreType.DMA((6,)),
        ],
        (COVER, 400_000),
        4 << 20,
    )(me, *[in_hbm(x) for x in (ids, row, field, weights)])
    far = neighbour(far)
    near = partner(near)
    others = []
    for k in range(1, chips):
        others.append(across(row if k == chips // 2 else mine, k))
    mine = jnp.concatenate([mine] + others, axis=0)
    theirs = partner(mine)

    extent = cells + 2 * halo
    still, answer = call(
        functools.partial(still_body, halo),
        [SMEM] + [VMEM] * 3,
        (f32(cells, LANES), f32(3 * halo, LANES)),
        [pltpu.VMEM((cells + 7 * halo + 2 * SUB, LANES), jnp.float32)] * 2,
        (COVER, 40_000_000),
        4 << 20,
    )(me, near, far, field)
    pivot_rows = pivots.reshape(-1, LANES)
    wall, permuted = call(
        functools.partial(wall_body, halo),
        [SMEM, SMEM] + [VMEM] * 9,
        (f32(extent, LANES), f32(*pivot_rows.shape)),
        [],
        (COVER, 40_000_000),
        4 << 20,
    )(me, ids, mine, theirs, own, near, far, still, answer, weights, pivot_rows)

    near_field = (comps, extent + 2 * SUB, width)
    pair = permuted + partner(permuted)
    pieces = [pair]
    for k in range(1, chips):
        pieces.append(across(pair, k))
    early = call(
        functools.partial(early_body, halo),
        [SMEM] + [VMEM] * 4,
        f32(*near_field),
        [pltpu.VMEM(near_field, jnp.float32)] * 2,
        (COVER, 4_000_000),
        8 << 20,
    )(me, near, far, field, wall)
    lower = call(
        functools.partial(lower_body, len(pieces)),
        [VMEM] * (len(pieces) + 1),
        f32(1, block),
        [pltpu.VMEM(pivot_rows.shape, jnp.float32)],
        (COVER, 1_000_000),
        4 << 20,
    )(*pieces, lower_inverse)
    total = lower
    for k in range(1, sections):
        pairs = [(i, i ^ k) for i in range(sections)]
        total = total + lax.ppermute(lower, "sec", pairs)
    both = jnp.concatenate([total, partner(total)], axis=0)
    middle = [both]
    for k in range(1, chips):
        middle.append(across(both, k))
    new_flow = call(
        functools.partial(late_body, halo),
        [VMEM],
        f32(comps, cells, width),
        [pltpu.VMEM(near_field, jnp.float32)] * 2,
        (COVER, 4_000_000),
        8 << 20,
    )(early)
    new_disp = call(
        functools.partial(upper_body, len(middle)),
        [SMEM] + [VMEM] * (len(middle) + 2),
        f32(1, block),
        [pltpu.VMEM((domains, block), jnp.float32)],
        (COVER, 1_000_000),
        4 << 20,
    )(me, *middle, row, upper_inverse)
    return (new_flow[None], new_disp.reshape(block))


def fits(mesh):
    chips, odd = divmod(mesh.shape["dom"], 2)
    sections = mesh.shape["sec"]
    powers = chips & (chips - 1) == 0 and sections & (sections - 1) == 0
    return odd == 0 and powers and 1 < chips <= 8 and sections <= 8


def body_for(mesh):
    def body(disp_coarse, support_ids, rbf_weights, flow, pivots, lower_inverse, upper_inverse):
        args = (disp_coarse, support_ids, rbf_weights, flow, pivots, lower_inverse, upper_inverse)
        block = disp_coarse.shape[0]
        cells, width = flow.shape[2:]
        halo = REACH * ITERS
        small = (
            block % width == 0
            and width % LANES == 0
            and cells % (4 * halo) == 0
            and halo == SUB
            and 2 * halo < GROUP
            and flow.shape[1] == 4
            and pivots.shape[0] % (SUB * LANES) == 0
            and support_ids.shape[2] <= SUB
        )
        return fast_shards(*args) if fits(mesh) and small else shards(*args)

    return body


def solution(mesh):
    return jax.shard_map(
        body_for(mesh),
        mesh=mesh,
        in_specs=(
            P("dom"),
            P("sec", "dom", None),
            P("sec", "dom", None, None, None),
            P("sec", None, "dom", None),
            P(),
            P("dom", None),
            P("dom", None),
        ),
        out_specs=(P("sec", None, "dom", None), P("dom")),
        check_vma=False,
    )
```
